32 devices in a mesh: sky: 8 (over z, y), batch: 4 (over x, core).
Axes of the slice: x: 2, y: 2, z: 4, core: 2. Of those that a mesh axis runs over, the one named last changes fastest.
Arguments:
- features: float32 [4, 8, 80, 1024], P('batch', 'sky'), may hold values from -0.1875 to 0.1875
- target: float32 [4, 8, 576, 1024], P('batch', 'sky'), may hold values from -2 to 2
- images: float32 [4, 8, 16, 80], P('batch', 'sky'), may hold values from -6 to 6
- layer_mask: int32 [4, 8, 16], P('batch', 'sky'), may hold values 0 or 1
- pair_list: int32 [4, 8, 9], P('batch', 'sky'), may hold values from 0 to 11, as said below
- ridge_weight: float32 [4, 8], P('batch', 'sky'), may hold values from 0.2 to 1
Outputs:
- transfer: float32 [4, 8, 720, 576], P('batch', 'sky')
- final_image: float32 [16, 96, 192], P(None, 'batch', 'sky')
The draws below stay inside these ranges and needn't reach their ends.
Inputs may be any that keep to these rules, and one draw needn't show every extreme that they name: `pair_list`: the 9 entries of each output stamp are distinct candidate numbers.
All inputs are finite; a program needn't handle non-finite values. No bound on the sum of `layer_mask` on one device may be relied on, other than what follows from the above.
Results may differ from the reference program's by a relative error of at most 0.0003.
Values sent between devices are 32-bit elements; how exact they have to be, the bound alone decides.
No kernel may reach another device: no remote copies, remote signals or barrier semaphores. Data moves between devices by JAX's collectives and lax.ppermute only.
A program may use at most 128 MiB of HBM per device.

```python
import math
import jax
import jax.numpy as jnp
from jax import lax

NPIX = 80
FEAT = 1024
SIDE = 24
LAYERS = 16
NSEL = 9
FADE = 4
ORDER = 720
NOUT_PIX = 576
CAND = 12
N_SKY = 8
N_BATCH = 4


def draw_pair_list(key, part):
    scores = jax.random.randint(key, (N_BATCH, N_SKY, CAND), 0, 65536) * CAND + jnp.arange(CAND, dtype=jnp.int32)
    ordering = jnp.argsort(scores, axis=-1, stable=True)
    return ordering[..., :NSEL].astype(jnp.int32)


def plant(array, stream_key, smallest, top_value):
    extent = array.shape
    spot = [jax.random.randint(jax.random.fold_in(stream_key, axis), (), 0, extent[axis]) for axis in range(len(extent))]
    array = array.at[tuple(spot)].set(smallest)
    longest = extent.index(max(extent))
    spot[longest] = (spot[longest] + 1) % extent[longest]
    return array.at[tuple(spot)].set(top_value)


def level_of(own_key, shape, split, smallest, top_value):
    def one(axis_at, blocks):
        steps = jax.random.uniform(jax.random.fold_in(jax.random.fold_in(own_key, 6), axis_at), (blocks,), jnp.float32, smallest / len(split), top_value / len(split))
        return jnp.repeat(jnp.exp(steps), shape[axis_at] // blocks).reshape((-1,) + (1,) * (len(shape) - axis_at - 1))

    gain = one(*split[0])
    for cut in split[1:]:
        gain = gain * one(*cut)
    return gain


def noise(rng, shape, scale, most, pieces=(), kind=jnp.bfloat16):
    loudness = level_of(rng, shape, pieces, -0.22, 0.18) if pieces else 1.0
    result = jax.random.normal(rng, shape, jnp.float32) * scale * loudness
    return jnp.minimum(jnp.maximum(result, -most), most).astype(kind)


def setup_inputs(seed: int = 0) -> dict:
    splits = jax.random.split(jax.random.key(seed), 7)
    features = noise(splits[0], (N_BATCH, N_SKY, NPIX, FEAT), FEAT ** -0.5, 0.1875, ((0, 4), (1, 8)), jnp.float32)
    target = noise(splits[1], (N_BATCH, N_SKY, NOUT_PIX, FEAT), 0.15, 2.0, ((0, 4), (1, 8)), jnp.float32)
    images = noise(splits[2], (N_BATCH, N_SKY, LAYERS, NPIX), 1.0, 6.0, ((0, 4), (1, 8)), jnp.float32)
    layer_mask = plant((jax.random.randint(splits[3], (N_BATCH, N_SKY, LAYERS), 0, 4) < 3).astype(jnp.int32), jax.random.fold_in(splits[3], 1), 0, 1)
    pair_list = draw_pair_list(jax.random.fold_in(splits[6], 71), 0)
    ridge_weight = jnp.clip(jnp.exp(math.log(1.0) - 1.609438 * jax.random.uniform(splits[5], (N_BATCH, N_SKY), jnp.float32) ** level_of(splits[5], (N_BATCH, N_SKY), ((0, 4), (1, 8)), -0.2, 0.2)), 0.2, 1.0)
    return {"features": features, "target": target, "images": images, "layer_mask": layer_mask, "pair_list": pair_list, "ridge_weight": ridge_weight}


precise = lax.Precision.HIGHEST

def reference(features, target, images, layer_mask, pair_list, ridge_weight):
    masked = images * layer_mask[..., None].astype(jnp.float32)
    padded_feat = jnp.pad(features, ((0, 0), (1, 1), (0, 0), (0, 0)))
    padded_image = jnp.pad(masked, ((0, 0), (1, 1), (0, 0), (0, 0)))

    def per_stamp(flat_index):
        batch_pos = flat_index // N_SKY
        sky_pos = flat_index % N_SKY
        window = lax.dynamic_slice_in_dim(padded_feat, sky_pos, 3, 1).reshape(CAND, NPIX, FEAT)
        image_window = lax.dynamic_slice_in_dim(padded_image, sky_pos, 3, 1).reshape(CAND, LAYERS, NPIX)
        chosen = pair_list[batch_pos, sky_pos]
        chosen_feat = window[chosen].reshape(ORDER, FEAT)
        chosen_image = image_window[chosen]
        system = jnp.dot(chosen_feat, chosen_feat.T, precision=precise)
        system = system + ridge_weight[batch_pos, sky_pos] * jnp.eye(ORDER, dtype=jnp.float32)
        right_sides = jnp.dot(chosen_feat, target[batch_pos, sky_pos].T, precision=precise)
        factor = jnp.linalg.cholesky(system)
        midway = lax.linalg.triangular_solve(factor, right_sides, left_side=True, lower=True)
        transfer = lax.linalg.triangular_solve(factor, midway, left_side=True, lower=True, transpose_a=True)
        coadded = jnp.einsum('kio,kli->lo', transfer.reshape(NSEL, NPIX, NOUT_PIX), chosen_image, precision=precise)
        return (transfer, coadded.reshape(LAYERS, SIDE, SIDE))
    transfer_all, coadded_all = lax.map(per_stamp, jnp.arange(N_BATCH * N_SKY, dtype=jnp.int32))
    transfer_all = transfer_all.reshape(N_BATCH, N_SKY, ORDER, NOUT_PIX)
    stamps_grid = coadded_all.reshape(N_BATCH, N_SKY, LAYERS, SIDE, SIDE)
    padded_grid = jnp.pad(stamps_grid, ((1, 1), (1, 1), (0, 0), (0, 0), (0, 0)))
    east_strip = padded_grid[1:-1, 2:, :, :, :FADE]
    west_strip = padded_grid[1:-1, :-2, :, :, SIDE - FADE:]
    south_strip = padded_grid[2:, 1:-1, :, :FADE, :]
    north_strip = padded_grid[:-2, 1:-1, :, SIDE - FADE:, :]
    fade_ramp = (jnp.arange(FADE, dtype=jnp.float32) + 1.0) / (FADE + 1.0)
    blended = stamps_grid
    blended = blended.at[..., :, SIDE - FADE:].add(fade_ramp * east_strip)
    blended = blended.at[..., :, :FADE].add(fade_ramp[::-1] * west_strip)
    blended = blended.at[..., SIDE - FADE:, :].add(fade_ramp[:, None] * south_strip)
    blended = blended.at[..., :FADE, :].add(fade_ramp[::-1][:, None] * north_strip)
    final_image = blended.transpose(2, 0, 3, 1, 4).reshape(LAYERS, N_BATCH * SIDE, N_SKY * SIDE)
    return (transfer_all, final_image)
```

```python
import functools
import jax
import jax.numpy as jnp
from jax import lax
from jax.experimental import pallas as pl
from jax.experimental.pallas import tpu as pltpu
from jax.sharding import PartitionSpec as P

f32 = jnp.float32
bf16 = jnp.bfloat16
LANE = 128
SUB = 8
FADE = 4


def split2(x):
    hi = x.astype(bf16)
    lo = (x - hi.astype(f32)).astype(bf16)
    return hi, lo


def dot(a, b, tb=False):
    dims = (((1,), (1 if tb else 0,)), ((), ()))
    return lax.dot_general(a, b, dims, preferred_element_type=f32)


def dot3(ah, al, bh, bl, tb=False):
    return dot(ah, bh, tb) + (dot(ah, bl, tb) + dot(al, bh, tb))


def panel_sweep(rows, q, sub, lane):
    base = q * SUB
    p = rows[q]
    cols = [jnp.broadcast_to(p[:, base + k : base + k + 1], (SUB, LANE)) for k in range(SUB)]
    inside = (lane >= base) & (lane < base + SUB)
    w = jnp.where(inside, jnp.where(lane - base == sub, 1.0, 0.0).astype(f32), p)
    for k in range(SUB):
        here = sub == k
        inv = 1.0 / jnp.broadcast_to(cols[k][k : k + 1, :], (SUB, LANE))
        h = jnp.where(here, -1.0, cols[k])
        for m in range(k + 1, SUB):
            r = jnp.broadcast_to(cols[m][k : k + 1, :], (SUB, LANE))
            cols[m] = jnp.where(here, 0.0, cols[m]) - (h * r) * inv
        r = jnp.broadcast_to(w[k : k + 1, :], (SUB, LANE))
        w = jnp.where(here, 0.0, w) - (h * r) * inv
    wk = [jnp.broadcast_to(w[k : k + 1, :], (SUB, LANE)) for k in range(SUB)]
    out = []
    count = len(rows)
    order = [(q + 1 + i) % count for i in range(count)]
    res = [None] * count
    for g in order:
        if g == q:
            res[g] = w
            continue
        a = rows[g]
        acc = [jnp.where(inside, 0.0, a), None]
        for k in range(SUB):
            t = jnp.broadcast_to(a[:, base + k : base + k + 1], (SUB, LANE)) * wk[k]
            s = k % 2
            acc[s] = (acc[s] - t) if acc[s] is not None else -t
        res[g] = acc[0] + acc[1]
    return res


def solve_kernel(sel_ref, ridge_ref, win_ref, img_ref, tgt_ref, out_ref, co_ref,
                 fsel, fh, fl, th, tl, s_ref, r_ref, sems, *, npix, nsel, feat, nout):
    order = npix * nsel
    nblk = -(-order // LANE)
    padded = nblk * LANE
    copies = []
    for k in range(nsel):
        cp = pltpu.make_async_copy(win_ref.at[sel_ref[k], pl.ds(0, npix)], fsel.at[pl.ds(k * npix, npix)], sems.at[k])
        cp.start()
        copies.append(cp)
    t = tgt_ref[...]
    hi, lo = split2(t)
    th[...] = hi
    tl[...] = lo
    if padded > order:
        fh[order:padded, :] = jnp.zeros((padded - order, feat), bf16)
        fl[order:padded, :] = jnp.zeros((padded - order, feat), bf16)
    for k in range(nsel):
        copies[k].wait()
        hi, lo = split2(fsel[k * npix : (k + 1) * npix, :])
        fh[k * npix : (k + 1) * npix, :] = hi
        fl[k * npix : (k + 1) * npix, :] = lo
    ridge = ridge_ref[0]
    sub = lax.broadcasted_iota(jnp.int32, (SUB, LANE), 0)
    lane = lax.broadcasted_iota(jnp.int32, (SUB, LANE), 1)

    def gram(c, width=1):
        lo_, hi_ = c * LANE, (c + width) * LANE
        g = dot3(fh[...], fl[...], fh[lo_:hi_, :], fl[lo_:hi_, :], True)
        for w in range(width):
            s_ref[c + w] = g[:, w * LANE : (w + 1) * LANE]

    def rhs():
        r_ref[...] = dot3(fh[...], fl[...], th[...], tl[...], True)

    def load_diag(c):
        top = c * LANE
        rows_here = min(order - top, LANE) // SUB
        rows = []
        for g in range(rows_here):
            a = s_ref[c, top + g * SUB : top + (g + 1) * SUB, :]
            rows.append(a + jnp.where(lane == sub + g * SUB, ridge, 0.0))
        return rows

    def apply(c, coef_h, coef_l, dh, dl, j, is_rhs=False):
        top = j * LANE
        size = min(order - top, LANE)
        if is_rhs:
            block = r_ref[top : top + size, :]
        else:
            block = s_ref[c, top : top + size, :]
        bh, bl = split2(block)
        w = dot3(dh, dl, bh, bl)
        wh, wl = split2(w)
        upd = dot3(coef_h, coef_l, wh, wl)
        if is_rhs:
            r_ref[...] = r_ref[...] - upd
            r_ref[top : top + size, :] = w
        else:
            s_ref[c] = s_ref[c] - upd
            s_ref[c, top : top + size, :] = w

    gram(0)
    work = []
    for c in range(1, nblk, 2):
        work.append(functools.partial(gram, c, min(2, nblk - c)))
    work.append(rhs)
    for j in range(nblk):
        rows = load_diag(j)
        count = len(rows)
        for q in range(count):
            rows = panel_sweep(rows, q, sub, lane)
            take = -(-len(work) // (count - q))
            for _ in range(take):
                work.pop(0)()
        while work:
            work.pop(0)()
        size = count * SUB
        d = jnp.concatenate(rows, axis=0)[:, :size] if size < LANE else jnp.concatenate(rows, axis=0)
        dh, dl = split2(d)
        coef = s_ref[j]
        if size < LANE:
            coef = coef[:, :size]
        ch, cl = split2(coef)
        if j + 1 < nblk:
            apply(j + 1, ch, cl, dh, dl, j)
        for c in range(j + 2, nblk):
            work.append(functools.partial(apply, c, ch, cl, dh, dl, j))
        work.append(functools.partial(apply, 0, ch, cl, dh, dl, j, True))
    while work:
        work.pop(0)()
    total = None
    for k in range(nsel):
        xh, xl = split2(r_ref[k * npix : (k + 1) * npix, :])
        ih, il = split2(img_ref[sel_ref[k]])
        part = dot3(ih, il, xh, xl)
        total = part if total is None else total + part
        out_ref[k * npix : (k + 1) * npix, :] = r_ref[k * npix : (k + 1) * npix, :]
    co_ref[...] = total


def solve(window, images, target, sel, ridge):
    npix, feat = images.shape[2], target.shape[1]
    nout = target.shape[0]
    nsel = sel.shape[0]
    order = npix * nsel
    nblk = -(-order // LANE)
    padded = nblk * LANE
    return pl.pallas_call(
        functools.partial(solve_kernel, npix=npix, nsel=nsel, feat=feat, nout=nout),
        out_shape=(
            jax.ShapeDtypeStruct((order, nout), f32),
            jax.ShapeDtypeStruct((images.shape[1], nout), f32),
        ),
        in_specs=[
            pl.BlockSpec(memory_space=pltpu.SMEM),
            pl.BlockSpec(memory_space=pltpu.SMEM),
            pl.BlockSpec(memory_space=pl.ANY),
            pl.BlockSpec(memory_space=pltpu.VMEM),
            pl.BlockSpec(memory_space=pltpu.VMEM),
        ],
        out_specs=(pl.BlockSpec(memory_space=pltpu.VMEM), pl.BlockSpec(memory_space=pltpu.VMEM)),
        scratch_shapes=[
            pltpu.VMEM((order, feat), f32),
            pltpu.VMEM((padded, feat), bf16),
            pltpu.VMEM((padded, feat), bf16),
            pltpu.VMEM((nout, feat), bf16),
            pltpu.VMEM((nout, feat), bf16),
            pltpu.VMEM((nblk, padded, LANE), f32),
            pltpu.VMEM((padded, nout), f32),
            pltpu.SemaphoreType.DMA((nsel,)),
        ],
        compiler_params=pltpu.CompilerParams(vmem_limit_bytes=60 << 20),
        name="solve",
    )(sel, ridge, window, images, target)


def swap(value, axis, bit):
    count = lax.axis_size(axis)
    return lax.ppermute(value, axis, [(i, i ^ bit) for i in range(count)])


def hop_two(value):
    count = lax.axis_size("sky")
    pairs = [(i, i + 2) for i in range(0, count - 2, 2)] + [(i, i - 2) for i in range(3, count, 2)]
    return lax.ppermute(value, "sky", pairs)


def gather_window(own):
    a1 = swap(own, "batch", 1)
    a2 = swap(own, "batch", 2)
    n0 = swap(own, "sky", 1)
    n2 = swap(n0, "batch", 2)
    d0 = hop_two(n0)
    d2 = swap(d0, "batch", 2)
    a3 = swap(a2, "batch", 1)
    n1 = swap(n0, "batch", 1)
    n3 = swap(n2, "batch", 1)
    d1 = swap(d0, "batch", 1)
    d3 = swap(d2, "batch", 1)
    return jnp.stack([own, a1, a2, a3, n0, n1, n2, n3, d0, d1, d2, d3])


def shift(value, axis, step):
    count = lax.axis_size(axis)
    return lax.ppermute(
        value, axis, [(i, i + step) for i in range(count) if 0 <= i + step < count]
    )


def local(features, target, images, layer_mask, pair_list, ridge_weight):
    npix, feat = features.shape[2:]
    layers = images.shape[2]
    nout = target.shape[2]
    side = int(round(nout**0.5))
    masked = (images * layer_mask[..., None].astype(f32)).reshape(layers, npix)
    extra = jnp.pad(masked.reshape(SUB, layers * npix // SUB), ((0, 0), (0, feat - layers * npix // SUB)))
    own = jnp.concatenate([features.reshape(npix, feat), extra], axis=0)
    window = gather_window(own)
    win_feat = window
    win_img = window[:, npix:, : layers * npix // SUB].reshape(-1, layers, npix)
    chosen = pair_list.reshape(-1)
    p, u = chosen // 3, chosen % 3
    odd = lax.axis_index("sky") % 2
    near = jnp.where(odd == 1, 0, 2)
    tile = jnp.where(u == 1, 0, jnp.where(u == near, 1, 2))
    slot = tile * 4 + (p ^ lax.axis_index("batch"))
    transfer, coadded = solve(win_feat, win_img, target.reshape(nout, feat), slot.astype(jnp.int32), ridge_weight.reshape(1))
    coadded = coadded.reshape(layers, side, side)
    east = shift(coadded[:, :, :FADE], "sky", -1)
    west = shift(coadded[:, :, side - FADE :], "sky", 1)
    south = shift(coadded[:, :FADE, :], "batch", -1)
    north = shift(coadded[:, side - FADE :, :], "batch", 1)
    ramp = (jnp.arange(FADE, dtype=f32) + 1.0) / (FADE + 1.0)
    back = ramp[::-1]
    rest = side - FADE
    blended = (
        coadded
        + jnp.pad(ramp * east, ((0, 0), (0, 0), (rest, 0)))
        + jnp.pad(back * west, ((0, 0), (0, 0), (0, rest)))
        + jnp.pad(ramp[:, None] * south, ((0, 0), (rest, 0), (0, 0)))
        + jnp.pad(back[:, None] * north, ((0, 0), (0, rest), (0, 0)))
    )
    return (transfer.reshape(1, 1, -1, nout), blended)


def solution(mesh):
    in_specs = (
        P("batch", "sky", None, None),
        P("batch", "sky", None, None),
        P("batch", "sky", None, None),
        P("batch", "sky", None),
        P("batch", "sky", None),
        P("batch", "sky"),
    )
    out_specs = (P("batch", "sky", None, None), P(None, "batch", "sky"))
    return jax.shard_map(local, mesh=mesh, in_specs=in_specs, out_specs=out_specs, check_vma=False)
```

```python
import functools

import jax
import jax.numpy as jnp
import numpy as np
from jax import lax
from jax.experimental import pallas as pl
from jax.experimental.pallas import tpu as pltpu
from jax.sharding import PartitionSpec as P

f32 = jnp.float32
bf16 = jnp.bfloat16
LANE = 128
SUB = 8
FADE = 4
PHASES = (3, 3, 3)
ARRIVED = (6, 10, 12)
FLIP = (0, 1, 2, 0, 3, 1, 2, 0, 3, 1, 2, 3)
TILE = (0, 0, 0, 1, 0, 1, 1, 2, 1, 2, 2, 2)


def split2(x):
    hi = x.astype(bf16)
    lo = (x - hi.astype(f32)).astype(bf16)
    return hi, lo


def dot(a, b, tb=False):
    dims = (((1,), (1 if tb else 0,)), ((), ()))
    return lax.dot_general(a, b, dims, preferred_element_type=f32)


def dot3(a, b, tb=False):
    return dot(a[0], b[0], tb) + (dot(a[0], b[1], tb) + dot(a[1], b[0], tb))


def panel_sweep(rows, q, sub, lane):
    base = q * SUB
    p = rows[q]
    cols = [
        jnp.where(lane >= 0, jnp.broadcast_to(p[:, base + k : base + k + 1], (SUB, LANE)), 0.0)
        for k in range(SUB)
    ]
    inside = (lane >= base) & (lane < base + SUB)
    w = jnp.where(inside, jnp.where(lane - base == sub, 1.0, 0.0).astype(f32), p)
    for k in range(SUB):
        here = sub == k
        inv = 1.0 / jnp.broadcast_to(cols[k][k : k + 1, :], (SUB, LANE))
        h = jnp.where(here, -1.0, cols[k])
        for m in range(k + 1, SUB):
            r = jnp.broadcast_to(cols[m][k : k + 1, :], (SUB, LANE))
            cols[m] = jnp.where(here, 0.0, cols[m]) - (h * r) * inv
        r = jnp.broadcast_to(w[k : k + 1, :], (SUB, LANE))
        w = jnp.where(here, 0.0, w) - (h * r) * inv
    wk = [jnp.broadcast_to(w[k : k + 1, :], (SUB, LANE)) for k in range(SUB)]
    count = len(rows)
    res = [None] * count
    for step in range(count):
        g = (q + 1 + step) % count
        if g == q:
            res[g] = w
            continue
        a = rows[g]
        acc = [jnp.where(inside, 0.0, a), None]
        for k in range(SUB):
            t = jnp.broadcast_to(a[:, base + k : base + k + 1], (SUB, LANE)) * wk[k]
            s = k % 2
            acc[s] = (acc[s] - t) if acc[s] is not None else -t
        res[g] = acc[0] + acc[1]
    return res


def pack_kernel(mask_ref, feat_in, img_in, out_ref, feat_ref, img_ref, sems):
    npix, feat = feat_ref.shape
    layers = img_ref.shape[0]
    blocks = feat // LANE
    loads = [
        pltpu.make_async_copy(feat_in.at[0, 0], feat_ref, sems.at[0]),
        pltpu.make_async_copy(img_in.at[0, 0], img_ref, sems.at[1]),
    ]
    for cp in loads:
        cp.start()
    row = lax.broadcasted_iota(jnp.int32, (layers, npix), 0)
    keep = jnp.zeros((layers, npix), f32)
    for i in range(layers):
        keep = jnp.where(row == i, mask_ref[0, 0, i].astype(f32), keep)
    for cp in loads:
        cp.wait()
    for c in range(blocks):
        out_ref[c * npix : (c + 1) * npix, :] = feat_ref[:, c * LANE : (c + 1) * LANE]
    tail = blocks * npix
    out_ref[tail : tail + layers, :] = jnp.zeros((layers, LANE), f32)
    out_ref[tail : tail + layers, 0:npix] = img_ref[...] * keep


def pack(features, images, layer_mask):
    npix, feat = features.shape[2:]
    layers = images.shape[2]
    vm = pl.BlockSpec(memory_space=pltpu.VMEM)
    hb = pl.BlockSpec(memory_space=pltpu.HBM)
    return pl.pallas_call(
        pack_kernel,
        out_shape=jax.ShapeDtypeStruct((feat // LANE * npix + layers, LANE), f32),
        in_specs=[pl.BlockSpec(memory_space=pltpu.SMEM), hb, hb],
        out_specs=vm,
        scratch_shapes=[
            pltpu.VMEM((npix, feat), f32),
            pltpu.VMEM((layers, npix), f32),
            pltpu.SemaphoreType.DMA((2,)),
        ],
        compiler_params=pltpu.CompilerParams(vmem_limit_bytes=8 << 20),
        name="pack",
    )(layer_mask, features, images)


def halve_kernel(t_ref, hi_ref, lo_ref):
    hi, lo = split2(t_ref[0, 0])
    hi_ref[...] = hi
    lo_ref[...] = lo


def halve(target):
    nout, feat = target.shape[2:]
    vm = pl.BlockSpec(memory_space=pltpu.VMEM)
    shape = jax.ShapeDtypeStruct((nout, feat), bf16)
    return pl.pallas_call(
        halve_kernel,
        out_shape=(shape, shape),
        in_specs=[vm],
        out_specs=(vm, vm),
        compiler_params=pltpu.CompilerParams(vmem_limit_bytes=16 << 20),
        name="halve",
    )(target)


def stack_left(x):
    hi, lo = split2(x)
    return jnp.concatenate([hi, hi, lo], axis=1)


def stack_right(x):
    hi, lo = split2(x)
    return jnp.concatenate([hi, lo, hi], axis=0)


def chunks(width, step=256):
    return [slice(at, min(at + step, width)) for at in range(0, width, step)]


def phase_kernel(*refs, done, narr, last, npix, layers, nout, side):
    refs = list(refs)
    take = lambda count: [refs.pop(0) for _ in range(count)]
    rank_ref, ridge_ref, odd_ref = take(3)
    if last:
        (mask_ref,) = take(1)
    arrs = take(narr)
    t_in = take(2)
    old_in = [tuple(take(2)) for _ in done]
    p_in, w_in = take(2) if done else (None, None)
    e = sum(done)
    if last:
        z_out, v_out, co_ref, near_ref, far_ref, pair_ref, mid_ref = take(7)
    else:
        fh_out, fl_out, p_out, w_out = take(4)
    fsel, fh_ref, fl_ref, s_ref, d_ref, r_ref, th, tl = take(8)
    sems, sem = take(2)
    l = fsel.shape[0]
    n = l * npix
    before = e * npix
    if not last:
        p_ref, w_ref = take(2)
    else:
        img_ref, img_sems = take(2)
    if done:
        old = [tuple(take(2)) for _ in done]
        old_p, old_w, v_ref = take(3)
    feat_blocks = fh_ref.shape[1] // LANE
    body = feat_blocks * npix

    def picks(t):
        r = rank_ref[t]
        return r, (r >= e) & (r < e + l)

    def copy(t, r):
        return pltpu.make_async_copy(arrs[t], fsel.at[r - e], sems.at[t])

    def copy_img(t, r):
        return pltpu.make_async_copy(arrs[t].at[pl.ds(body, layers)], img_ref.at[r], img_sems.at[t])

    for t in range(narr):
        r, hit = picks(t)

        @pl.when(hit)
        def _():
            copy(t, r).start()

    pairs = []
    for src, dst in zip(old_in, old if done else []):
        pairs += [(src[0], dst[0]), (src[1], dst[1])]
    early = len(pairs)
    if done:
        pairs += [(p_in, old_p), (w_in, old_w)]
    pairs += [(t_in[0], th), (t_in[1], tl)]
    loads = [pltpu.make_async_copy(x, y, sem.at[i]) for i, (x, y) in enumerate(pairs)]
    for cp in loads:
        cp.start()
    if last:
        for t in range(narr):
            r = rank_ref[t]

            @pl.when(r >= 0)
            def _():
                copy_img(t, r).start()

    for t in range(narr):
        r, hit = picks(t)

        @pl.when(hit)
        def _():
            copy(t, r).wait()

    for i in range(l):
        for c in range(feat_blocks):
            hi, lo = split2(fsel[i, c * npix : (c + 1) * npix, :])
            fh_ref[i * npix : (i + 1) * npix, c * LANE : (c + 1) * LANE] = hi
            fl_ref[i * npix : (i + 1) * npix, c * LANE : (c + 1) * LANE] = lo
    stores = []
    at = len(pairs)
    if not last:
        stores = [
            pltpu.make_async_copy(fh_ref, fh_out, sem.at[at]),
            pltpu.make_async_copy(fl_ref, fl_out, sem.at[at + 1]),
        ]
        for cp in stores:
            cp.start()
    first = early + (1 if done else 0)
    for cp in loads[:first]:
        cp.wait()
    mine = (fh_ref[...], fl_ref[...])
    ridge = ridge_ref[0, 0]
    sub = lax.broadcasted_iota(jnp.int32, (SUB, LANE), 0)
    lane = lax.broadcasted_iota(jnp.int32, (SUB, LANE), 1)
    system = dot3(mine, mine, True)
    cross = []
    if done:
        tops = [sum(done[:i]) * npix for i in range(len(done) + 1)]
        parts = [(x[...], y[...]) for x, y in old]
        gel = jnp.concatenate([dot3(part, mine, True) for part in parts], axis=0)
        v = dot3(split2(old_p[...]), split2(gel))
        v_ref[...] = v
        for i, part in enumerate(parts):
            g = split2(dot3(mine, part, True))
            cross.append((slice(tops[i], tops[i + 1]), g))
        for rows, g in cross:
            system = system - dot3(g, split2(v[rows, :]))
    d_ref[:, 0:npix] = system[0:npix, 0:npix]
    for c in range(l):
        s_ref[c, :, 0:npix] = system[:, c * npix : (c + 1) * npix]

    for cp in loads[first:]:
        cp.wait()
    if last:
        for t in range(narr):
            r = rank_ref[t]

            @pl.when(r >= 0)
            def _():
                copy_img(t, r).wait()

    work = []
    feat = feat_blocks * LANE

    def right_sides(cut, deep, fresh):
        part = dot3(
            (fh_ref[:, deep], fl_ref[:, deep]), (th[cut, deep], tl[cut, deep]), True
        )
        r_ref[:, cut] = part if fresh else r_ref[:, cut] + part

    def cross_right(cut, rows, g):
        r_ref[:, cut] = r_ref[:, cut] - dot3(g, split2(old_w[rows, cut]))

    for cut in chunks(nout):
        for deep in chunks(feat):
            work.append(functools.partial(right_sides, cut, deep, deep.start == 0))
        for rows, g in cross:
            work.append(functools.partial(cross_right, cut, rows, g))

    picture = {}
    if last:

        def base(cut):
            total = None
            for i in range(e):
                part = dot(
                    stack_left(img_ref[i][:, 0:npix]), stack_right(old_w[i * npix : (i + 1) * npix, cut])
                )
                total = part if total is None else total + part
            picture[cut.start] = total

        def effective():
            ours = jnp.concatenate([img_ref[e + i][:, 0:npix] for i in range(l)], axis=1)
            for i in range(e):
                ours = ours - dot(
                    stack_left(img_ref[i][:, 0:npix]), stack_right(v_ref[i * npix : (i + 1) * npix, :])
                )
            picture["rest"] = split2(ours)

        for cut in chunks(nout):
            work.append(functools.partial(base, cut))
        work.append(effective)

    def update(c, coef, d, j):
        rows = slice(j * npix, (j + 1) * npix)
        w = dot(d, stack_right(s_ref[c, rows, 0:npix]))
        s_ref[c, :, 0:npix] = s_ref[c, :, 0:npix] - dot(coef, stack_right(w))
        s_ref[c, rows, 0:npix] = w

    def update_right(coef, d, j, cut):
        rows = slice(j * npix, (j + 1) * npix)
        w = dot(d, stack_right(r_ref[rows, cut]))
        r_ref[:, cut] = r_ref[:, cut] - dot(coef, stack_right(w))
        r_ref[rows, cut] = w

    def update_own(coef, full, j):
        rows = slice(j * npix, (j + 1) * npix)
        s_ref[j, :, 0:npix] = -dot(coef, stack_right(full))
        s_ref[j, rows, 0:npix] = full

    for j in range(l):
        cut = slice(j * npix, (j + 1) * npix)
        after = slice((j + 1) * npix, (j + 2) * npix)
        rows = []
        for g in range(npix // SUB):
            at_row = slice(g * SUB, (g + 1) * SUB)
            rows.append(d_ref[at_row, :] + jnp.where(lane == sub + g * SUB, ridge, 0.0))
        count = len(rows)
        for q in range(count):
            rows = panel_sweep(rows, q, sub, lane)
            for _ in range(-(-len(work) // (count - q))):
                work.pop(0)()
        while work:
            work.pop(0)()
        full = jnp.concatenate(rows, axis=0)[:, :npix]
        if j + 1 < l:
            w = dot3(split2(full), split2(s_ref[j + 1, cut, 0:npix]))
            step = dot3(split2(s_ref[j, after, 0:npix]), split2(w))
            d_ref[:, 0:npix] = s_ref[j + 1, after, 0:npix] - step
        d = stack_left(full)
        coef = stack_left(s_ref[j, :, 0:npix])
        for c in list(range(j + 1, l)) + list(range(j)):
            if c > j or not last:
                work.append(functools.partial(update, c, coef, d, j))
        for part in chunks(nout):
            work.append(functools.partial(update_right, coef, d, j, part))
        if not last:
            work.append(functools.partial(update_own, coef, full, j))
    while work:
        work.pop(0)()
    z = r_ref[...]
    z2 = split2(z)
    if last:
        stores = [
            pltpu.make_async_copy(r_ref, z_out, sem.at[at]),
            pltpu.make_async_copy(v_ref, v_out, sem.at[at + 1]),
        ]
        for cp in stores:
            cp.start()
        base_total = jnp.concatenate([picture[cut.start] for cut in chunks(nout)], axis=1)
        total = base_total + dot3(picture["rest"], z2)
        send(total, co_ref, near_ref, far_ref, pair_ref, mid_ref, mask_ref, odd_ref, side)
        for cp in stores:
            cp.wait()
        return
    q_flat = jnp.concatenate([s_ref[c, :, 0:npix] for c in range(l)], axis=1)
    w_ref[before : before + n, :] = z
    if done:
        v2 = split2(v_ref[...])
        w_ref[0:before, :] = old_w[...] - dot3(v2, z2)
        q2 = split2(q_flat)
        vq = dot3(v2, q2)
        second = dot3(q2, v2, True)
        first = old_p[...] + dot3(split2(vq), v2, True)
        p_ref[0:before, :] = jnp.concatenate([first, -vq], axis=1)
        p_ref[before : before + n, :] = jnp.concatenate([-second, q_flat], axis=1)
    else:
        p_ref[...] = q_flat
    more = [
        pltpu.make_async_copy(p_ref, p_out, sem.at[at + 2]),
        pltpu.make_async_copy(w_ref, w_out, sem.at[at + 3]),
    ]
    for cp in more:
        cp.start()
    for cp in stores + more:
        cp.wait()


def send(total, co_ref, near_ref, far_ref, pair_ref, mid_ref, mask_ref, odd_ref, side):
    layers, nout = total.shape
    rest = side - FADE
    span = FADE * side
    co_ref[...] = total
    none = jnp.zeros((layers, rest), f32)
    to_west = jnp.concatenate([none, total[:, : nout - rest]], axis=1) * mask_ref[0:1, :]
    to_east = jnp.concatenate([total[:, rest:], none], axis=1) * mask_ref[1:2, :]
    to_north = total[:, 0:span] * mask_ref[2:3, 0:span]
    to_south = total[:, nout - span :] * mask_ref[3:4, 0:span]
    sky_odd, batch_odd = odd_ref[0] == 1, odd_ref[1] == 1
    near_ref[...] = jnp.where(sky_odd, to_west, to_east)
    far_ref[...] = jnp.where(sky_odd, to_east, to_west)
    pair_ref[...] = jnp.where(batch_odd, to_north, to_south)
    mid_ref[...] = jnp.where(batch_odd, to_south, to_north)


def fade_masks(nout, side):
    ramp = (np.arange(FADE, dtype=np.float32) + np.float32(1.0)) / np.float32(FADE + 1.0)
    column = np.arange(nout) % side
    rest = side - FADE
    masks = np.zeros((4, nout), np.float32)
    masks[0] = np.where(column >= rest, ramp[np.maximum(column - rest, 0)], 0.0)
    masks[1] = np.where(column < FADE, ramp[::-1][np.minimum(column, FADE - 1)], 0.0)
    masks[2, : FADE * side] = np.repeat(ramp, side)
    masks[3, : FADE * side] = np.repeat(ramp[::-1], side)
    return masks


def phase(number, rank, ridge, odd, masks, arrs, t2, old, state, shapes):
    npix, layers, nout, side, feat = shapes
    done = PHASES[:number]
    l = PHASES[number]
    last = number == len(PHASES) - 1
    e = sum(done)
    n, size = l * npix, (e + l) * npix
    vm = pl.BlockSpec(memory_space=pltpu.VMEM)
    sm = pl.BlockSpec(memory_space=pltpu.SMEM)
    hb = pl.BlockSpec(memory_space=pltpu.HBM)
    args = [rank, ridge, odd]
    specs = [sm, sm, sm]
    if last:
        args += [masks]
        specs += [vm]
    args += list(arrs) + list(t2)
    for pair in old:
        args += list(pair)
    if done:
        args += list(state)
    specs += [hb] * (len(args) - len(specs))
    real = lambda *shape: jax.ShapeDtypeStruct(shape, f32)
    half = jax.ShapeDtypeStruct((n, feat), bf16)
    if last:
        outs = (
            real(n, nout),
            real(e * npix, n),
            real(layers, nout),
            real(layers, nout),
            real(layers, nout),
            real(layers, FADE * side),
            real(layers, FADE * side),
        )
        out_specs = (hb, hb, vm, vm, vm, vm, vm)
    else:
        outs = (half, half, real(size, size), real(size, nout))
        out_specs = (hb, hb, hb, hb)
    fh = pltpu.VMEM((n, feat), bf16)
    tgt = pltpu.VMEM((nout, feat), bf16)
    scratch = [
        pltpu.VMEM((l,) + arrs[0].shape, f32),
        fh,
        fh,
        pltpu.VMEM((l, n, LANE), f32),
        pltpu.VMEM((npix, LANE), f32),
        pltpu.VMEM((n, nout), f32),
        tgt,
        tgt,
        pltpu.SemaphoreType.DMA((len(arrs),)),
        pltpu.SemaphoreType.DMA((2 * len(done) + 8,)),
    ]
    if last:
        scratch += [
            pltpu.VMEM((e + l, layers, LANE), f32),
            pltpu.SemaphoreType.DMA((len(arrs),)),
        ]
    else:
        scratch += [pltpu.VMEM((size, size), f32), pltpu.VMEM((size, nout), f32)]
    if done:
        for count in done:
            scratch += [pltpu.VMEM((count * npix, feat), bf16)] * 2
        scratch += [
            pltpu.VMEM((e * npix, e * npix), f32),
            pltpu.VMEM((e * npix, nout), f32),
            pltpu.VMEM((e * npix, n), f32),
        ]
    return pl.pallas_call(
        functools.partial(
            phase_kernel,
            done=done,
            narr=len(arrs),
            last=last,
            npix=npix,
            layers=layers,
            nout=nout,
            side=side,
        ),
        out_shape=outs,
        in_specs=specs,
        out_specs=out_specs,
        scratch_shapes=scratch,
        compiler_params=pltpu.CompilerParams(vmem_limit_bytes=40 << 20),
        cost_estimate=pl.CostEstimate(
            flops=2_000_000_000 * l, transcendentals=0, bytes_accessed=4_000_000
        ),
        name="phase%d" % number,
    )(*args)


def close_kernel(pos_ref, w_in, v_in, z_in, out_ref, w_ref, v_ref, x_ref, sems):
    before = w_ref.shape[0]
    n = z_in.shape[0]
    count = pos_ref.shape[0]
    npix = (before + n) // count
    loads = [
        pltpu.make_async_copy(v_in, v_ref, sems.at[0]),
        pltpu.make_async_copy(z_in, x_ref.at[pl.ds(before, n)], sems.at[1]),
        pltpu.make_async_copy(w_in, w_ref, sems.at[2]),
    ]
    for cp in loads:
        cp.start()
    for cp in loads:
        cp.wait()
    z2 = split2(x_ref[before : before + n, :])
    x_ref[0:before, :] = w_ref[...] - dot3(split2(v_ref[...]), z2)
    for i in range(count):
        src = pl.multiple_of(pos_ref[i] * npix, SUB)
        out_ref[i * npix : (i + 1) * npix, :] = x_ref[pl.ds(src, npix), :]


def close(pos, w, v, z):
    before, nout = w.shape
    n = z.shape[0]
    hb = pl.BlockSpec(memory_space=pltpu.HBM)
    vm = pl.BlockSpec(memory_space=pltpu.VMEM)
    return pl.pallas_call(
        close_kernel,
        out_shape=jax.ShapeDtypeStruct((before + n, nout), f32),
        in_specs=[pl.BlockSpec(memory_space=pltpu.SMEM), hb, hb, hb],
        out_specs=vm,
        scratch_shapes=[
            pltpu.VMEM((before, nout), f32),
            pltpu.VMEM((before, n), f32),
            pltpu.VMEM((before + n, nout), f32),
            pltpu.SemaphoreType.DMA((3,)),
        ],
        compiler_params=pltpu.CompilerParams(vmem_limit_bytes=20 << 20),
        cost_estimate=pl.CostEstimate(
            flops=500_000_000, transcendentals=0, bytes_accessed=6_000_000
        ),
        name="close",
    )(pos, w, v, z)


def blend_kernel(odd_ref, co_ref, near_ref, far_ref, pair_ref, mid_ref, out_ref):
    layers, side, _ = out_ref.shape
    nout = co_ref.shape[1]
    span = FADE * side
    batch_odd = odd_ref[1] == 1
    pair, mid = pair_ref[...], mid_ref[...]
    south = jnp.where(batch_odd, mid, pair)
    north = jnp.where(batch_odd, pair, mid)
    none = jnp.zeros((layers, nout - 2 * span), f32)
    total = co_ref[...] + near_ref[...] + far_ref[...] + jnp.concatenate([north, none, south], axis=1)
    for r in range(side):
        out_ref[:, r, :] = total[:, r * side : (r + 1) * side]


def blend(odd, co, strips, side):
    vm = pl.BlockSpec(memory_space=pltpu.VMEM)
    return pl.pallas_call(
        blend_kernel,
        out_shape=jax.ShapeDtypeStruct((co.shape[0], side, side), f32),
        in_specs=[pl.BlockSpec(memory_space=pltpu.SMEM)] + [vm] * 5,
        out_specs=vm,
        compiler_params=pltpu.CompilerParams(vmem_limit_bytes=8 << 20),
        name="blend",
    )(odd, co, *strips)


def swap(value, axis, bit):
    count = lax.axis_size(axis)
    return lax.ppermute(value, axis, [(i, i ^ bit) for i in range(count)])


def between(value, axis):
    count = lax.axis_size(axis)
    pairs = [(i, i + 1) for i in range(1, count - 1, 2)]
    return lax.ppermute(value, axis, pairs + [(j, i) for i, j in pairs])


def hop_two(value):
    count = lax.axis_size("sky")
    pairs = [(i, i + 2) for i in range(0, count - 2, 2)] + [(i, i - 2) for i in range(3, count, 2)]
    return lax.ppermute(value, "sky", pairs)


def local(features, target, images, layer_mask, pair_list, ridge_weight):
    npix, feat = features.shape[2:]
    layers = images.shape[2]
    nout = target.shape[2]
    side = int(round(nout**0.5))
    shapes = (npix, layers, nout, side, feat)
    sky_at, batch_at = lax.axis_index("sky"), lax.axis_index("batch")
    own = pack(features, images, layer_mask)
    n0 = swap(own, "sky", 1)
    a2 = swap(own, "batch", 2)
    a1 = swap(own, "batch", 1)
    t2 = halve(target)
    chosen = pair_list.reshape(-1)
    odd = sky_at % 2
    tiles = jnp.asarray(TILE, jnp.int32)
    column = jnp.where(tiles == 0, 1, jnp.where((tiles == 1) == (odd == 0), 2, 0))
    names = 3 * (jnp.asarray(FLIP, jnp.int32) ^ batch_at) + column
    match = (names[:, None] == chosen[None, :]).astype(jnp.int32)
    hit = jnp.sum(match, axis=1)
    order = jnp.arange(names.shape[0])
    count = jnp.sum(jnp.where(order[None, :] < order[:, None], hit[None, :], 0), axis=1)
    rank = jnp.where(hit > 0, count, -1).astype(jnp.int32)
    pos = jnp.sum(match * count[:, None], axis=0).astype(jnp.int32)
    parity = jnp.stack([odd, batch_at % 2]).astype(jnp.int32)

    masks = jnp.asarray(fade_masks(nout, side))
    common = (rank, ridge_weight, parity, masks)
    d0 = hop_two(n0)
    n2 = swap(n0, "batch", 2)
    a3 = swap(a2, "batch", 1)
    n1 = swap(n0, "batch", 1)
    arrs = [own, a1, a2, n0, a3, n1]
    fa_h, fa_l, p, w = phase(0, *common, arrs, t2, [], None, shapes)
    n2, d0, fa_h = lax.optimization_barrier((n2, d0, fa_h))
    d2 = swap(d0, "batch", 2)
    n3 = swap(n2, "batch", 1)
    d1 = swap(d0, "batch", 1)
    arrs += [n2, d0, n3, d1]
    fb_h, fb_l, p, w = phase(1, *common, arrs, t2, [(fa_h, fa_l)], (p, w), shapes)
    d2, fb_h = lax.optimization_barrier((d2, fb_h))
    d3 = swap(d2, "batch", 1)
    arrs += [d2, d3]
    olds = [(fa_h, fa_l), (fb_h, fb_l)]
    z, v, co, near, far, pair, mid = phase(2, *common, arrs, t2, olds, (p, w), shapes)
    near = swap(near, "sky", 1)
    far = between(far, "sky")
    pair = swap(pair, "batch", 1)
    mid = between(mid, "batch")
    transfer = close(pos, w, v, z)
    image = blend(parity, co, (near, far, pair, mid), side)
    return (transfer.reshape(1, 1, -1, nout), image)


def solution(mesh):
    in_specs = (
        P("batch", "sky", None, None),
        P("batch", "sky", None, None),
        P("batch", "sky", None, None),
        P("batch", "sky", None),
        P("batch", "sky", None),
        P("batch", "sky"),
    )
    out_specs = (P("batch", "sky", None, None), P(None, "batch", "sky"))
    return jax.shard_map(local, mesh=mesh, in_specs=in_specs, out_specs=out_specs, check_vma=False)
```

```python
import functools

import jax
import jax.numpy as jnp
import numpy as np
from jax import lax
from jax.experimental import pallas as pl
from jax.experimental.pallas import tpu as pltpu
from jax.sharding import PartitionSpec as P

f32 = jnp.float32
bf16 = jnp.bfloat16
LANE = 128
SUB = 8
FADE = 4
PHASES = (3, 3, 3)
ARRIVED = (6, 10, 12)
FLIP = (0, 1, 2, 0, 3, 1, 2, 0, 3, 1, 2, 3)
TILE = (0, 0, 0, 1, 0, 1, 1, 2, 1, 2, 2, 2)


def split2(x):
    hi = x.astype(bf16)
    lo = (x - hi.astype(f32)).astype(bf16)
    return hi, lo


def dot(a, b, tb=False):
    dims = (((1,), (1 if tb else 0,)), ((), ()))
    return lax.dot_general(a, b, dims, preferred_element_type=f32)


def dot3(a, b, tb=False):
    return dot(a[0], b[0], tb) + (dot(a[0], b[1], tb) + dot(a[1], b[0], tb))


def panel_sweep(rows, q, sub, lane):
    base = q * SUB
    p = rows[q]
    wide = lambda x: jnp.broadcast_to(x, (SUB, LANE))
    cols = [jnp.where(lane >= 0, wide(p[:, base + k : base + k + 1]), 0.0) for k in range(SUB)]
    inside = (lane >= base) & (lane < base + SUB)
    w = jnp.where(inside, jnp.where(lane - base == sub, 1.0, 0.0).astype(f32), p)
    for k in range(0, SUB, 2):
        first, second = sub == k, sub == k + 1
        both = first | second
        a, d = wide(cols[k][k : k + 1]), wide(cols[k][k + 1 : k + 2])
        b, c = wide(cols[k + 1][k : k + 1]), wide(cols[k + 1][k + 1 : k + 2])
        r = 1.0 / (a * c - b * d)
        h1 = jnp.where(first, -1.0, jnp.where(second, 0.0, cols[k]))
        h2 = jnp.where(second, -1.0, jnp.where(first, 0.0, cols[k + 1]))

        def step(x):
            r1, r2 = wide(x[k : k + 1]), wide(x[k + 1 : k + 2])
            t = h1 * (c * r1 - b * r2) + h2 * (a * r2 - d * r1)
            return jnp.where(both, 0.0, x) - t * r

        for m in range(k + 2, SUB):
            cols[m] = step(cols[m])
        w = step(w)
    wk = [wide(w[k : k + 1]) for k in range(SUB)]
    count = len(rows)
    res = [None] * count
    for step_at in range(count):
        g = (q + 1 + step_at) % count
        if g == q:
            res[g] = w
            continue
        x = rows[g]
        terms = [wide(x[:, base + k : base + k + 1]) * wk[k] for k in range(SUB)]
        while len(terms) > 1:
            terms = [terms[i] + terms[i + 1] for i in range(0, len(terms), 2)]
        res[g] = jnp.where(inside, 0.0, x) - terms[0]
    return res


def pack_kernel(mask_ref, feat_in, img_in, out_ref, img_ref, sems):
    npix, feat = feat_in.shape[2:]
    layers = img_ref.shape[0]
    blocks = feat // LANE
    first = pltpu.make_async_copy(img_in.at[0, 0], img_ref, sems.at[blocks])
    first.start()
    loads = [
        pltpu.make_async_copy(
            feat_in.at[0, 0, :, pl.ds(c * LANE, LANE)],
            out_ref.at[pl.ds(c * npix, npix)],
            sems.at[c],
        )
        for c in range(blocks)
    ]
    for cp in loads:
        cp.start()
    row = lax.broadcasted_iota(jnp.int32, (layers, npix), 0)
    keep = jnp.zeros((layers, npix), f32)
    for i in range(layers):
        keep = jnp.where(row == i, mask_ref[0, 0, i].astype(f32), keep)
    tail = blocks * npix
    out_ref[tail : tail + layers, :] = jnp.zeros((layers, LANE), f32)
    first.wait()
    out_ref[tail : tail + layers, 0:npix] = img_ref[...] * keep
    for cp in loads:
        cp.wait()


def pack(features, images, layer_mask):
    npix, feat = features.shape[2:]
    layers = images.shape[2]
    vm = pl.BlockSpec(memory_space=pltpu.VMEM)
    hb = pl.BlockSpec(memory_space=pltpu.HBM)
    outside = lambda x: pltpu.with_memory_space_constraint(x, pltpu.HBM)
    return pl.pallas_call(
        pack_kernel,
        out_shape=jax.ShapeDtypeStruct((feat // LANE * npix + layers, LANE), f32),
        in_specs=[pl.BlockSpec(memory_space=pltpu.SMEM), hb, hb],
        out_specs=vm,
        scratch_shapes=[
            pltpu.VMEM((layers, npix), f32),
            pltpu.SemaphoreType.DMA((feat // LANE + 1,)),
        ],
        compiler_params=pltpu.CompilerParams(vmem_limit_bytes=8 << 20),
        name="pack",
    )(outside(layer_mask), outside(features), outside(images))


def halve_kernel(t_ref, hi_ref, lo_ref):
    hi, lo = split2(t_ref[0, 0])
    hi_ref[...] = hi
    lo_ref[...] = lo


def halve(target):
    nout, feat = target.shape[2:]
    vm = pl.BlockSpec(memory_space=pltpu.VMEM)
    shape = jax.ShapeDtypeStruct((nout, feat), bf16)
    return pl.pallas_call(
        halve_kernel,
        out_shape=(shape, shape),
        in_specs=[vm],
        out_specs=(vm, vm),
        compiler_params=pltpu.CompilerParams(vmem_limit_bytes=16 << 20),
        name="halve",
    )(target)


def stack_left(x):
    hi, lo = split2(x)
    return jnp.concatenate([hi, hi, lo], axis=1)


def stack_right(x):
    hi, lo = split2(x)
    return jnp.concatenate([hi, lo, hi], axis=0)


def chunks(width, step=256):
    return [slice(at, min(at + step, width)) for at in range(0, width, step)]


def phase_kernel(*refs, done, narr, last, npix, layers, nout, side):
    refs = list(refs)
    take = lambda count: [refs.pop(0) for _ in range(count)]
    rank_ref, ridge_ref, odd_ref = take(3)
    if last:
        (mask_ref,) = take(1)
    arrs = dict(zip(range(sum(done), narr), take(narr - sum(done))))
    th, tl = take(2)
    old = [tuple(take(2)) for _ in done]
    old_p, old_w = take(2) if done else (None, None)
    e = sum(done)
    old_img = take(len(done)) if last else []
    if last:
        r_ref, v_ref, co_ref, near_ref, far_ref, pair_ref, mid_ref = take(7)
        fh_ref, fl_ref, s_ref, d_ref, img_ref = take(5)
    else:
        fh_ref, fl_ref, p_ref, w_ref, img_ref = take(5)
        s_ref, d_ref, r_ref = take(3)
        if done:
            (v_ref,) = take(1)
    n = fh_ref.shape[0]
    l = n // npix
    before = e * npix
    feat_blocks = fh_ref.shape[1] // LANE
    body = feat_blocks * npix

    for t in arrs:
        r = rank_ref[t]

        @pl.when((r >= e) & (r < e + l))
        def _():
            to = pl.ds(pl.multiple_of((r - e) * npix, 2 * SUB), npix)
            for c in range(feat_blocks):
                hi, lo = split2(arrs[t][c * npix : (c + 1) * npix, :])
                fh_ref[to, c * LANE : (c + 1) * LANE] = hi
                fl_ref[to, c * LANE : (c + 1) * LANE] = lo
            img_ref[r - e] = arrs[t][body : body + layers, :]


    mine_h, mine_l = fh_ref[...], fl_ref[...]
    ridge = ridge_ref[0, 0]
    sub = lax.broadcasted_iota(jnp.int32, (SUB, LANE), 0)
    lane = lax.broadcasted_iota(jnp.int32, (SUB, LANE), 1)
    pieces = []
    for xh, xl in old + [(fh_ref, fl_ref)]:
        xh, xl = xh[...], xl[...]
        both = dot(jnp.concatenate([xh, xl], axis=0), mine_h, True)
        pieces.append(both[: xh.shape[0]] + (both[xh.shape[0] :] + dot(xh, mine_l, True)))
    system = pieces[-1]
    cross = []
    if done:
        tops = [sum(done[:i]) * npix for i in range(len(done) + 1)]
        gel = jnp.concatenate(pieces[:-1], axis=0)
        v = dot3(split2(old_p[...]), split2(gel))
        v_ref[...] = v
        for i in range(len(done)):
            rows = slice(tops[i], tops[i + 1])
            cross.append((rows, split2(gel[rows].T)))
        for rows, g in cross:
            system = system - dot3(g, split2(v[rows]))
    d_ref[:, 0:npix] = system[0:npix, 0:npix]
    for c in range(l):
        s_ref[c, :, 0:npix] = system[:, c * npix : (c + 1) * npix]

    work = []
    feat = feat_blocks * LANE

    def right_sides(cut, deep, fresh):
        part = dot3(
            (fh_ref[:, deep], fl_ref[:, deep]), (th[cut, deep], tl[cut, deep]), True
        )
        r_ref[:, cut] = part if fresh else r_ref[:, cut] + part

    def cross_right(cut, rows, g):
        r_ref[:, cut] = r_ref[:, cut] - dot3(g, split2(old_w[rows, cut]))

    for cut in chunks(nout):
        for deep in chunks(feat):
            work.append(functools.partial(right_sides, cut, deep, deep.start == 0))
        for rows, g in cross:
            work.append(functools.partial(cross_right, cut, rows, g))

    picture = {}
    if last:
        faces = [ref[i][:, 0:npix] for ref, count in zip(old_img, done) for i in range(count)]
        faces += [img_ref[i][:, 0:npix] for i in range(l)]

        def base(cut):
            total = None
            for i in range(e):
                part = dot(
                    stack_left(faces[i]), stack_right(old_w[i * npix : (i + 1) * npix, cut])
                )
                total = part if total is None else total + part
            picture[cut.start] = total

        def effective():
            ours = jnp.concatenate(faces[e:], axis=1)
            for i in range(e):
                ours = ours - dot(
                    stack_left(faces[i]), stack_right(v_ref[i * npix : (i + 1) * npix, :])
                )
            picture["rest"] = split2(ours)

        later = [functools.partial(base, cut) for cut in chunks(nout)] + [effective]
    else:
        later = []

    def update(c, coef, d, j):
        rows = slice(j * npix, (j + 1) * npix)
        w = dot(d, stack_right(s_ref[c, rows, 0:npix]))
        s_ref[c, :, 0:npix] = s_ref[c, :, 0:npix] - dot(coef, stack_right(w))
        s_ref[c, rows, 0:npix] = w

    def update_right(coef, d, j, cut):
        rows = slice(j * npix, (j + 1) * npix)
        w = dot(d, stack_right(r_ref[rows, cut]))
        r_ref[:, cut] = r_ref[:, cut] - dot(coef, stack_right(w))
        r_ref[rows, cut] = w

    def update_own(coef, full, j):
        rows = slice(j * npix, (j + 1) * npix)
        s_ref[j, :, 0:npix] = -dot(coef, stack_right(full))
        s_ref[j, rows, 0:npix] = full

    for j in range(l):
        cut = slice(j * npix, (j + 1) * npix)
        after = slice((j + 1) * npix, (j + 2) * npix)
        rows = []
        for g in range(npix // SUB):
            at_row = slice(g * SUB, (g + 1) * SUB)
            rows.append(d_ref[at_row, :] + jnp.where(lane == sub + g * SUB, ridge, 0.0))
        count = len(rows)
        for q in range(count):
            rows = panel_sweep(rows, q, sub, lane)
            for _ in range(-(-len(work) // (count - q))):
                work.pop(0)()
        while work:
            work.pop(0)()
        full = jnp.concatenate(rows, axis=0)[:, :npix]
        if j + 1 < l:
            w = dot3(split2(full), split2(s_ref[j + 1, cut, 0:npix]))
            step = dot3(split2(s_ref[j, after, 0:npix]), split2(w))
            d_ref[:, 0:npix] = s_ref[j + 1, after, 0:npix] - step
        d = stack_left(full)
        coef = stack_left(s_ref[j, :, 0:npix])
        for c in list(range(j + 1, l)) + list(range(j)):
            if c > j or not last:
                work.append(functools.partial(update, c, coef, d, j))
        for part in chunks(nout):
            work.append(functools.partial(update_right, coef, d, j, part))
        if not last:
            work.append(functools.partial(update_own, coef, full, j))
        work += later
        later = []
    while work:
        work.pop(0)()
    z = r_ref[...]
    z2 = split2(z)
    if last:
        base_total = jnp.concatenate([picture[cut.start] for cut in chunks(nout)], axis=1)
        total = base_total + dot3(picture["rest"], z2)
        send(total, co_ref, near_ref, far_ref, pair_ref, mid_ref, mask_ref, odd_ref, side)
        return
    q_flat = jnp.concatenate([s_ref[c, :, 0:npix] for c in range(l)], axis=1)
    w_ref[before : before + n, :] = z
    if done:
        v2 = split2(v_ref[...])
        w_ref[0:before, :] = old_w[...] - dot3(v2, z2)
        q2 = split2(q_flat)
        vq = dot3(v2, q2)
        second = dot3(q2, v2, True)
        first = old_p[...] + dot3(split2(vq), v2, True)
        p_ref[0:before, :] = jnp.concatenate([first, -vq], axis=1)
        p_ref[before : before + n, :] = jnp.concatenate([-second, q_flat], axis=1)
    else:
        p_ref[...] = q_flat


def send(total, co_ref, near_ref, far_ref, pair_ref, mid_ref, mask_ref, odd_ref, side):
    layers, nout = total.shape
    rest = side - FADE
    span = FADE * side
    co_ref[...] = total
    none = jnp.zeros((layers, rest), f32)
    to_west = jnp.concatenate([none, total[:, : nout - rest]], axis=1) * mask_ref[0:1, :]
    to_east = jnp.concatenate([total[:, rest:], none], axis=1) * mask_ref[1:2, :]
    to_north = total[:, 0:span] * mask_ref[2:3, 0:span]
    to_south = total[:, nout - span :] * mask_ref[3:4, 0:span]
    sky_odd, batch_odd = odd_ref[0] == 1, odd_ref[1] == 1
    near_ref[...] = jnp.where(sky_odd, to_west, to_east)
    far_ref[...] = jnp.where(sky_odd, to_east, to_west)
    pair_ref[...] = jnp.where(batch_odd, to_north, to_south)
    mid_ref[...] = jnp.where(batch_odd, to_south, to_north)


def fade_masks(nout, side):
    ramp = (np.arange(FADE, dtype=np.float32) + np.float32(1.0)) / np.float32(FADE + 1.0)
    column = np.arange(nout) % side
    rest = side - FADE
    masks = np.zeros((4, nout), np.float32)
    masks[0] = np.where(column >= rest, ramp[np.maximum(column - rest, 0)], 0.0)
    masks[1] = np.where(column < FADE, ramp[::-1][np.minimum(column, FADE - 1)], 0.0)
    masks[2, : FADE * side] = np.repeat(ramp, side)
    masks[3, : FADE * side] = np.repeat(ramp[::-1], side)
    return masks


def phase(number, rank, ridge, odd, masks, arrs, t2, old, state, faces, shapes):
    npix, layers, nout, side, feat = shapes
    done = PHASES[:number]
    l = PHASES[number]
    last = number == len(PHASES) - 1
    e = sum(done)
    n, size = l * npix, (e + l) * npix
    vm = pl.BlockSpec(memory_space=pltpu.VMEM)
    sm = pl.BlockSpec(memory_space=pltpu.SMEM)
    args = [rank, ridge, odd]
    specs = [sm, sm, sm]
    if last:
        args += [masks]
    args += list(arrs[e:]) + list(t2)
    for pair in old:
        args += list(pair)
    if done:
        args += list(state)
    if last:
        args += list(faces)
    specs += [vm] * (len(args) - len(specs))
    real = lambda *shape: jax.ShapeDtypeStruct(shape, f32)
    half = jax.ShapeDtypeStruct((n, feat), bf16)
    if last:
        outs = (
            real(n, nout),
            real(e * npix, n),
            real(layers, nout),
            real(layers, nout),
            real(layers, nout),
            real(layers, FADE * side),
            real(layers, FADE * side),
        )
        scratch = [pltpu.VMEM((n, feat), bf16)] * 2
    else:
        outs = (half, half, real(size, size), real(size, nout), real(l, layers, LANE))
        scratch = []
    scratch += [pltpu.VMEM((l, n, LANE), f32), pltpu.VMEM((npix, LANE), f32)]
    if last:
        scratch += [pltpu.VMEM((l, layers, LANE), f32)]
    else:
        scratch += [pltpu.VMEM((n, nout), f32)]
        if done:
            scratch += [pltpu.VMEM((e * npix, n), f32)]
    out_specs = tuple(vm for _ in outs)
    return pl.pallas_call(
        functools.partial(
            phase_kernel,
            done=done,
            narr=len(arrs),
            last=last,
            npix=npix,
            layers=layers,
            nout=nout,
            side=side,
        ),
        out_shape=outs,
        in_specs=specs,
        out_specs=out_specs,
        scratch_shapes=scratch,
        compiler_params=pltpu.CompilerParams(vmem_limit_bytes=16 << 20),
        cost_estimate=pl.CostEstimate(
            flops=2_000_000_000 * l, transcendentals=0, bytes_accessed=4_000_000
        ),
        name="phase%d" % number,
    )(*args)


def close_kernel(pos_ref, w_ref, v_ref, z_ref, out_ref, x_ref):
    before = w_ref.shape[0]
    n = z_ref.shape[0]
    count = pos_ref.shape[0]
    npix = (before + n) // count
    z = z_ref[...]
    x_ref[before : before + n, :] = z
    x_ref[0:before, :] = w_ref[...] - dot3(split2(v_ref[...]), split2(z))
    for i in range(count):
        src = pl.multiple_of(pos_ref[i] * npix, SUB)
        out_ref[i * npix : (i + 1) * npix, :] = x_ref[pl.ds(src, npix), :]


def close(pos, w, v, z):
    before, nout = w.shape
    n = z.shape[0]
    vm = pl.BlockSpec(memory_space=pltpu.VMEM)
    return pl.pallas_call(
        close_kernel,
        out_shape=jax.ShapeDtypeStruct((before + n, nout), f32),
        in_specs=[pl.BlockSpec(memory_space=pltpu.SMEM), vm, vm, vm],
        out_specs=vm,
        scratch_shapes=[pltpu.VMEM((before + n, nout), f32)],
        compiler_params=pltpu.CompilerParams(vmem_limit_bytes=20 << 20),
        cost_estimate=pl.CostEstimate(
            flops=500_000_000, transcendentals=0, bytes_accessed=6_000_000
        ),
        name="close",
    )(pos, w, v, z)


def blend_kernel(odd_ref, co_ref, near_ref, far_ref, pair_ref, mid_ref, out_ref):
    layers, side, _ = out_ref.shape
    nout = co_ref.shape[1]
    span = FADE * side
    batch_odd = odd_ref[1] == 1
    pair, mid = pair_ref[...], mid_ref[...]
    south = jnp.where(batch_odd, mid, pair)
    north = jnp.where(batch_odd, pair, mid)
    none = jnp.zeros((layers, nout - 2 * span), f32)
    total = co_ref[...] + near_ref[...] + far_ref[...] + jnp.concatenate([north, none, south], axis=1)
    for r in range(side):
        out_ref[:, r, :] = total[:, r * side : (r + 1) * side]


def blend(odd, co, strips, side):
    vm = pl.BlockSpec(memory_space=pltpu.VMEM)
    return pl.pallas_call(
        blend_kernel,
        out_shape=jax.ShapeDtypeStruct((co.shape[0], side, side), f32),
        in_specs=[pl.BlockSpec(memory_space=pltpu.SMEM)] + [vm] * 5,
        out_specs=vm,
        compiler_params=pltpu.CompilerParams(vmem_limit_bytes=8 << 20),
        name="blend",
    )(odd, co, *strips)


def swap(value, axis, bit):
    count = lax.axis_size(axis)
    return lax.ppermute(value, axis, [(i, i ^ bit) for i in range(count)])


def between(value, axis):
    count = lax.axis_size(axis)
    pairs = [(i, i + 1) for i in range(1, count - 1, 2)]
    return lax.ppermute(value, axis, pairs + [(j, i) for i, j in pairs])


def hop_two(value):
    count = lax.axis_size("sky")
    pairs = [(i, i + 2) for i in range(0, count - 2, 2)] + [(i, i - 2) for i in range(3, count, 2)]
    return lax.ppermute(value, "sky", pairs)


def local(features, target, images, layer_mask, pair_list, ridge_weight):
    npix, feat = features.shape[2:]
    layers = images.shape[2]
    nout = target.shape[2]
    side = int(round(nout**0.5))
    shapes = (npix, layers, nout, side, feat)
    sky_at, batch_at = lax.axis_index("sky"), lax.axis_index("batch")
    own = pack(features, images, layer_mask)
    n0 = swap(own, "sky", 1)
    a2 = swap(own, "batch", 2)
    a1 = swap(own, "batch", 1)
    t2 = halve(target)
    chosen = pair_list.reshape(-1)
    odd = sky_at % 2
    tiles = jnp.asarray(TILE, jnp.int32)
    column = jnp.where(tiles == 0, 1, jnp.where((tiles == 1) == (odd == 0), 2, 0))
    names = 3 * (jnp.asarray(FLIP, jnp.int32) ^ batch_at) + column
    match = (names[:, None] == chosen[None, :]).astype(jnp.int32)
    hit = jnp.sum(match, axis=1)
    order = jnp.arange(names.shape[0])
    count = jnp.sum(jnp.where(order[None, :] < order[:, None], hit[None, :], 0), axis=1)
    rank = jnp.where(hit > 0, count, -1).astype(jnp.int32)
    pos = jnp.sum(match * count[:, None], axis=0).astype(jnp.int32)
    parity = jnp.stack([odd, batch_at % 2]).astype(jnp.int32)

    masks = jnp.asarray(fade_masks(nout, side))
    common = (rank, ridge_weight, parity, masks)
    d0 = hop_two(n0)
    n2 = swap(n0, "batch", 2)
    a3 = swap(a2, "batch", 1)
    n1 = swap(n0, "batch", 1)
    arrs = [own, a1, a2, n0, a3, n1]
    fa_h, fa_l, p, w, ia = phase(0, *common, arrs, t2, [], None, [], shapes)
    n2, d0, fa_h = lax.optimization_barrier((n2, d0, fa_h))
    d2 = swap(d0, "batch", 2)
    n3 = swap(n2, "batch", 1)
    d1 = swap(d0, "batch", 1)
    arrs += [n2, d0, n3]
    fb_h, fb_l, p, w, ib = phase(1, *common, arrs, t2, [(fa_h, fa_l)], (p, w), [], shapes)
    d2, fb_h = lax.optimization_barrier((d2, fb_h))
    d3 = swap(d2, "batch", 1)
    arrs += [d1, d2, d3]
    olds = [(fa_h, fa_l), (fb_h, fb_l)]
    z, v, co, near, far, pair, mid = phase(
        2, *common, arrs, t2, olds, (p, w), [ia, ib], shapes
    )
    near = swap(near, "sky", 1)
    far = between(far, "sky")
    pair = swap(pair, "batch", 1)
    mid = between(mid, "batch")
    transfer = close(pos, w, v, z)
    image = blend(parity, co, (near, far, pair, mid), side)
    return (transfer.reshape(1, 1, -1, nout), image)


def solution(mesh):
    in_specs = (
        P("batch", "sky", None, None),
        P("batch", "sky", None, None),
        P("batch", "sky", None, None),
        P("batch", "sky", None),
        P("batch", "sky", None),
        P("batch", "sky"),
    )
    out_specs = (P("batch", "sky", None, None), P(None, "batch", "sky"))
    return jax.shard_map(local, mesh=mesh, in_specs=in_specs, out_specs=out_specs, check_vma=False)
```

```python
import functools

import jax
import jax.numpy as jnp
import numpy as np
from jax import lax
from jax.experimental import pallas as pl
from jax.experimental.pallas import tpu as pltpu
from jax.sharding import PartitionSpec as P

f32 = jnp.float32
bf16 = jnp.bfloat16
LANE = 128
SUB = 8
FADE = 4
PHASES = (3, 3, 3)
ARRIVED = (6, 10, 12)
FLIP = (0, 1, 2, 0, 3, 1, 2, 0, 3, 1, 2, 3)
TILE = (0, 0, 0, 1, 0, 1, 1, 2, 1, 2, 2, 2)


def split2(x):
    hi = x.astype(bf16)
    lo = (x - hi.astype(f32)).astype(bf16)
    return hi, lo


def dot(a, b, tb=False):
    dims = (((1,), (1 if tb else 0,)), ((), ()))
    return lax.dot_general(a, b, dims, preferred_element_type=f32)


def dot3(a, b, tb=False):
    return dot(a[0], b[0], tb) + (dot(a[0], b[1], tb) + dot(a[1], b[0], tb))


def panel_sweep(rows, q, sub, lane):
    base = q * SUB
    p = rows[q]
    wide = lambda x: jnp.broadcast_to(x, (SUB, LANE))
    cols = [jnp.where(lane >= 0, wide(p[:, base + k : base + k + 1]), 0.0) for k in range(SUB)]
    inside = (lane >= base) & (lane < base + SUB)
    w = jnp.where(inside, jnp.where(lane - base == sub, 1.0, 0.0).astype(f32), p)
    for k in range(0, SUB, 2):
        first, second = sub == k, sub == k + 1
        both = first | second
        a, d = wide(cols[k][k : k + 1]), wide(cols[k][k + 1 : k + 2])
        b, c = wide(cols[k + 1][k : k + 1]), wide(cols[k + 1][k + 1 : k + 2])
        r = 1.0 / (a * c - b * d)
        h1 = jnp.where(first, -1.0, jnp.where(second, 0.0, cols[k]))
        h2 = jnp.where(second, -1.0, jnp.where(first, 0.0, cols[k + 1]))

        def step(x):
            r1, r2 = wide(x[k : k + 1]), wide(x[k + 1 : k + 2])
            t = h1 * (c * r1 - b * r2) + h2 * (a * r2 - d * r1)
            return jnp.where(both, 0.0, x) - t * r

        for m in range(k + 2, SUB):
            cols[m] = step(cols[m])
        w = step(w)
    wk = [wide(w[k : k + 1]) for k in range(SUB)]
    count = len(rows)
    res = [None] * count
    for step_at in range(count):
        g = (q + 1 + step_at) % count
        if g == q:
            res[g] = w
            continue
        x = rows[g]
        terms = [wide(x[:, base + k : base + k + 1]) * wk[k] for k in range(SUB)]
        while len(terms) > 1:
            terms = [terms[i] + terms[i + 1] for i in range(0, len(terms), 2)]
        res[g] = jnp.where(inside, 0.0, x) - terms[0]
    return res


def pack_kernel(mask_ref, feat_in, img_in, out_ref, img_ref, sems):
    npix, feat = feat_in.shape[2:]
    layers = img_ref.shape[0]
    blocks = feat // LANE
    first = pltpu.make_async_copy(img_in.at[0, 0], img_ref, sems.at[blocks])
    first.start()
    loads = [
        pltpu.make_async_copy(
            feat_in.at[0, 0, :, pl.ds(c * LANE, LANE)],
            out_ref.at[pl.ds(c * npix, npix)],
            sems.at[c],
        )
        for c in range(blocks)
    ]
    for cp in loads:
        cp.start()
    row = lax.broadcasted_iota(jnp.int32, (layers, npix), 0)
    keep = jnp.zeros((layers, npix), f32)
    for i in range(layers):
        keep = jnp.where(row == i, mask_ref[0, 0, i].astype(f32), keep)
    tail = blocks * npix
    out_ref[tail : tail + layers, :] = jnp.zeros((layers, LANE), f32)
    first.wait()
    out_ref[tail : tail + layers, 0:npix] = img_ref[...] * keep
    for cp in loads:
        cp.wait()


def pack(features, images, layer_mask):
    npix, feat = features.shape[2:]
    layers = images.shape[2]
    vm = pl.BlockSpec(memory_space=pltpu.VMEM)
    hb = pl.BlockSpec(memory_space=pltpu.HBM)
    outside = lambda x: pltpu.with_memory_space_constraint(x, pltpu.HBM)
    return pl.pallas_call(
        pack_kernel,
        out_shape=jax.ShapeDtypeStruct((feat // LANE * npix + layers, LANE), f32),
        in_specs=[pl.BlockSpec(memory_space=pltpu.SMEM), hb, hb],
        out_specs=vm,
        scratch_shapes=[
            pltpu.VMEM((layers, npix), f32),
            pltpu.SemaphoreType.DMA((feat // LANE + 1,)),
        ],
        compiler_params=pltpu.CompilerParams(vmem_limit_bytes=8 << 20),
        name="pack",
    )(outside(layer_mask), outside(features), outside(images))


def halve_kernel(t_ref, hi_ref, lo_ref):
    hi, lo = split2(t_ref[0, 0])
    hi_ref[...] = hi
    lo_ref[...] = lo


def halve(target):
    nout, feat = target.shape[2:]
    vm = pl.BlockSpec(memory_space=pltpu.VMEM)
    shape = jax.ShapeDtypeStruct((nout, feat), bf16)
    return pl.pallas_call(
        halve_kernel,
        out_shape=(shape, shape),
        in_specs=[vm],
        out_specs=(vm, vm),
        compiler_params=pltpu.CompilerParams(vmem_limit_bytes=16 << 20),
        name="halve",
    )(target)


def stack_left(x):
    hi, lo = split2(x)
    return jnp.concatenate([hi, hi, lo], axis=1)


def stack_right(x):
    hi, lo = split2(x)
    return jnp.concatenate([hi, lo, hi], axis=0)


def chunks(width, step=256):
    return [slice(at, min(at + step, width)) for at in range(0, width, step)]


def phase_kernel(*refs, done, narr, last, npix, layers, nout, side):
    refs = list(refs)
    take = lambda count: [refs.pop(0) for _ in range(count)]
    rank_ref, ridge_ref, odd_ref = take(3)
    if last:
        (mask_ref,) = take(1)
    arrs = dict(zip(range(sum(done), narr), take(narr - sum(done))))
    th, tl = take(2)
    old = [tuple(take(2)) for _ in done]
    old_p, old_w = take(2) if done else (None, None)
    e = sum(done)
    old_img = take(len(done)) if last else []
    if last:
        r_ref, v_ref, co_ref, near_ref, far_ref, pair_ref, mid_ref = take(7)
        fh_ref, fl_ref, s_ref, d_ref, img_ref = take(5)
    else:
        fh_ref, fl_ref, p_ref, w_ref, img_ref = take(5)
        s_ref, d_ref, r_ref = take(3)
        if done:
            (v_ref,) = take(1)
    n = fh_ref.shape[0]
    l = n // npix
    before = e * npix
    feat_blocks = fh_ref.shape[1] // LANE
    body = feat_blocks * npix

    for t in arrs:
        r = rank_ref[t]

        @pl.when((r >= e) & (r < e + l))
        def _():
            to = pl.ds(pl.multiple_of((r - e) * npix, 2 * SUB), npix)
            for c in range(feat_blocks):
                hi, lo = split2(arrs[t][c * npix : (c + 1) * npix, :])
                fh_ref[to, c * LANE : (c + 1) * LANE] = hi
                fl_ref[to, c * LANE : (c + 1) * LANE] = lo
            img_ref[r - e] = arrs[t][body : body + layers, :]


    mine_h, mine_l = fh_ref[...], fl_ref[...]
    ridge = ridge_ref[0, 0]
    sub = lax.broadcasted_iota(jnp.int32, (SUB, LANE), 0)
    lane = lax.broadcasted_iota(jnp.int32, (SUB, LANE), 1)
    pieces = []
    for xh, xl in old + [(fh_ref, fl_ref)]:
        xh, xl = xh[...], xl[...]
        both = dot(jnp.concatenate([xh, xl], axis=0), mine_h, True)
        pieces.append(both[: xh.shape[0]] + (both[xh.shape[0] :] + dot(xh, mine_l, True)))
    system = pieces[-1]
    cross = []
    if done:
        tops = [sum(done[:i]) * npix for i in range(len(done) + 1)]
        gel = jnp.concatenate(pieces[:-1], axis=0)
        v = dot3(split2(old_p[...]), split2(gel))
        v_ref[...] = v
        for i in range(len(done)):
            rows = slice(tops[i], tops[i + 1])
            cross.append((rows, split2(gel[rows].T)))
        for rows, g in cross:
            system = system - dot3(g, split2(v[rows]))
    d_ref[:, 0:npix] = system[0:npix, 0:npix]
    for c in range(l):
        s_ref[c, :, 0:npix] = system[:, c * npix : (c + 1) * npix]

    work = []
    feat = feat_blocks * LANE

    def right_sides(cut, deep, fresh):
        part = dot3(
            (fh_ref[:, deep], fl_ref[:, deep]), (th[cut, deep], tl[cut, deep]), True
        )
        r_ref[:, cut] = part if fresh else r_ref[:, cut] + part

    def cross_right(cut, rows, g):
        r_ref[:, cut] = r_ref[:, cut] - dot3(g, split2(old_w[rows, cut]))

    for cut in chunks(nout):
        for deep in chunks(feat, feat):
            work.append(functools.partial(right_sides, cut, deep, deep.start == 0))
        for rows, g in cross:
            work.append(functools.partial(cross_right, cut, rows, g))

    picture = {}
    if last:
        faces = [ref[i][:, 0:npix] for ref, count in zip(old_img, done) for i in range(count)]
        faces += [img_ref[i][:, 0:npix] for i in range(l)]

        def base(cut):
            total = None
            for i in range(e):
                part = dot(
                    stack_left(faces[i]), stack_right(old_w[i * npix : (i + 1) * npix, cut])
                )
                total = part if total is None else total + part
            picture[cut.start] = total

        def effective():
            ours = jnp.concatenate(faces[e:], axis=1)
            for i in range(e):
                ours = ours - dot(
                    stack_left(faces[i]), stack_right(v_ref[i * npix : (i + 1) * npix, :])
                )
            picture["rest"] = split2(ours)

        later = [functools.partial(base, cut) for cut in chunks(nout)] + [effective]
    else:
        later = []

    def update(c, coef, d, j):
        rows = slice(j * npix, (j + 1) * npix)
        w = dot(d, stack_right(s_ref[c, rows, 0:npix]))
        s_ref[c, :, 0:npix] = s_ref[c, :, 0:npix] - dot(coef, stack_right(w))
        s_ref[c, rows, 0:npix] = w

    def update_right(coef, d, j, cut):
        rows = slice(j * npix, (j + 1) * npix)
        w = dot(d, stack_right(r_ref[rows, cut]))
        r_ref[:, cut] = r_ref[:, cut] - dot(coef, stack_right(w))
        r_ref[rows, cut] = w

    def update_own(coef, full, j):
        rows = slice(j * npix, (j + 1) * npix)
        s_ref[j, :, 0:npix] = -dot(coef, stack_right(full))
        s_ref[j, rows, 0:npix] = full

    for j in range(l):
        cut = slice(j * npix, (j + 1) * npix)
        after = slice((j + 1) * npix, (j + 2) * npix)
        rows = []
        for g in range(npix // SUB):
            at_row = slice(g * SUB, (g + 1) * SUB)
            rows.append(d_ref[at_row, :] + jnp.where(lane == sub + g * SUB, ridge, 0.0))
        count = len(rows)
        for q in range(count):
            rows = panel_sweep(rows, q, sub, lane)
            for _ in range(-(-len(work) // (count - q))):
                work.pop(0)()
        while work:
            work.pop(0)()
        full = jnp.concatenate(rows, axis=0)[:, :npix]
        if j + 1 < l:
            w = dot3(split2(full), split2(s_ref[j + 1, cut, 0:npix]))
            step = dot3(split2(s_ref[j, after, 0:npix]), split2(w))
            d_ref[:, 0:npix] = s_ref[j + 1, after, 0:npix] - step
        d = stack_left(full)
        coef = stack_left(s_ref[j, :, 0:npix])
        for c in list(range(j + 1, l)) + list(range(j)):
            if c > j or not last:
                work.append(functools.partial(update, c, coef, d, j))
        for part in chunks(nout):
            work.append(functools.partial(update_right, coef, d, j, part))
        if not last:
            work.append(functools.partial(update_own, coef, full, j))
        work += later
        later = []
    while work:
        work.pop(0)()
    z = r_ref[...]
    z2 = split2(z)
    if last:
        base_total = jnp.concatenate([picture[cut.start] for cut in chunks(nout)], axis=1)
        total = base_total + dot3(picture["rest"], z2)
        send(total, co_ref, near_ref, far_ref, pair_ref, mid_ref, mask_ref, odd_ref, side)
        return
    q_flat = jnp.concatenate([s_ref[c, :, 0:npix] for c in range(l)], axis=1)
    w_ref[before : before + n, :] = z
    if done:
        v2 = split2(v_ref[...])
        w_ref[0:before, :] = old_w[...] - dot3(v2, z2)
        q2 = split2(q_flat)
        vq = dot3(v2, q2)
        second = dot3(q2, v2, True)
        first = old_p[...] + dot3(split2(vq), v2, True)
        p_ref[0:before, :] = jnp.concatenate([first, -vq], axis=1)
        p_ref[before : before + n, :] = jnp.concatenate([-second, q_flat], axis=1)
    else:
        p_ref[...] = q_flat


def send(total, co_ref, near_ref, far_ref, pair_ref, mid_ref, mask_ref, odd_ref, side):
    layers, nout = total.shape
    rest = side - FADE
    span = FADE * side
    co_ref[...] = total
    none = jnp.zeros((layers, rest), f32)
    to_west = jnp.concatenate([none, total[:, : nout - rest]], axis=1) * mask_ref[0:1, :]
    to_east = jnp.concatenate([total[:, rest:], none], axis=1) * mask_ref[1:2, :]
    to_north = total[:, 0:span] * mask_ref[2:3, 0:span]
    to_south = total[:, nout - span :] * mask_ref[3:4, 0:span]
    sky_odd, batch_odd = odd_ref[0] == 1, odd_ref[1] == 1
    near_ref[...] = jnp.where(sky_odd, to_west, to_east)
    far_ref[...] = jnp.where(sky_odd, to_east, to_west)
    pair_ref[...] = jnp.where(batch_odd, to_north, to_south)
    mid_ref[...] = jnp.where(batch_odd, to_south, to_north)


def fade_masks(nout, side):
    ramp = (np.arange(FADE, dtype=np.float32) + np.float32(1.0)) / np.float32(FADE + 1.0)
    column = np.arange(nout) % side
    rest = side - FADE
    masks = np.zeros((4, nout), np.float32)
    masks[0] = np.where(column >= rest, ramp[np.maximum(column - rest, 0)], 0.0)
    masks[1] = np.where(column < FADE, ramp[::-1][np.minimum(column, FADE - 1)], 0.0)
    masks[2, : FADE * side] = np.repeat(ramp, side)
    masks[3, : FADE * side] = np.repeat(ramp[::-1], side)
    return masks


def phase(number, rank, ridge, odd, masks, arrs, t2, old, state, faces, shapes):
    npix, layers, nout, side, feat = shapes
    done = PHASES[:number]
    l = PHASES[number]
    last = number == len(PHASES) - 1
    e = sum(done)
    n, size = l * npix, (e + l) * npix
    vm = pl.BlockSpec(memory_space=pltpu.VMEM)
    sm = pl.BlockSpec(memory_space=pltpu.SMEM)
    args = [rank, ridge, odd]
    specs = [sm, sm, sm]
    if last:
        args += [masks]
    args += list(arrs[e:]) + list(t2)
    for pair in old:
        args += list(pair)
    if done:
        args += list(state)
    if last:
        args += list(faces)
    specs += [vm] * (len(args) - len(specs))
    real = lambda *shape: jax.ShapeDtypeStruct(shape, f32)
    half = jax.ShapeDtypeStruct((n, feat), bf16)
    if last:
        outs = (
            real(n, nout),
            real(e * npix, n),
            real(layers, nout),
            real(layers, nout),
            real(layers, nout),
            real(layers, FADE * side),
            real(layers, FADE * side),
        )
        scratch = [pltpu.VMEM((n, feat), bf16)] * 2
    else:
        outs = (half, half, real(size, size), real(size, nout), real(l, layers, LANE))
        scratch = []
    scratch += [pltpu.VMEM((l, n, LANE), f32), pltpu.VMEM((npix, LANE), f32)]
    if last:
        scratch += [pltpu.VMEM((l, layers, LANE), f32)]
    else:
        scratch += [pltpu.VMEM((n, nout), f32)]
        if done:
            scratch += [pltpu.VMEM((e * npix, n), f32)]
    out_specs = tuple(vm for _ in outs)
    return pl.pallas_call(
        functools.partial(
            phase_kernel,
            done=done,
            narr=len(arrs),
            last=last,
            npix=npix,
            layers=layers,
            nout=nout,
            side=side,
        ),
        out_shape=outs,
        in_specs=specs,
        out_specs=out_specs,
        scratch_shapes=scratch,
        compiler_params=pltpu.CompilerParams(vmem_limit_bytes=16 << 20),
        cost_estimate=pl.CostEstimate(
            flops=2_000_000_000 * l, transcendentals=0, bytes_accessed=4_000_000
        ),
        name="phase%d" % number,
    )(*args)


def close_kernel(pos_ref, w_ref, v_ref, z_ref, out_ref, x_ref):
    before = w_ref.shape[0]
    n = z_ref.shape[0]
    count = pos_ref.shape[0]
    npix = (before + n) // count
    z = z_ref[...]
    x_ref[before : before + n, :] = z
    x_ref[0:before, :] = w_ref[...] - dot3(split2(v_ref[...]), split2(z))
    for i in range(count):
        src = pl.multiple_of(pos_ref[i] * npix, SUB)
        out_ref[i * npix : (i + 1) * npix, :] = x_ref[pl.ds(src, npix), :]


def close(pos, w, v, z):
    before, nout = w.shape
    n = z.shape[0]
    vm = pl.BlockSpec(memory_space=pltpu.VMEM)
    return pl.pallas_call(
        close_kernel,
        out_shape=jax.ShapeDtypeStruct((before + n, nout), f32),
        in_specs=[pl.BlockSpec(memory_space=pltpu.SMEM), vm, vm, vm],
        out_specs=vm,
        scratch_shapes=[pltpu.VMEM((before + n, nout), f32)],
        compiler_params=pltpu.CompilerParams(vmem_limit_bytes=20 << 20),
        cost_estimate=pl.CostEstimate(
            flops=500_000_000, transcendentals=0, bytes_accessed=6_000_000
        ),
        name="close",
    )(pos, w, v, z)


def blend_kernel(odd_ref, co_ref, near_ref, far_ref, pair_ref, mid_ref, out_ref):
    layers, side, _ = out_ref.shape
    nout = co_ref.shape[1]
    span = FADE * side
    batch_odd = odd_ref[1] == 1
    pair, mid = pair_ref[...], mid_ref[...]
    south = jnp.where(batch_odd, mid, pair)
    north = jnp.where(batch_odd, pair, mid)
    none = jnp.zeros((layers, nout - 2 * span), f32)
    total = co_ref[...] + near_ref[...] + far_ref[...] + jnp.concatenate([north, none, south], axis=1)
    for r in range(side):
        out_ref[:, r, :] = total[:, r * side : (r + 1) * side]


def blend(odd, co, strips, side):
    vm = pl.BlockSpec(memory_space=pltpu.VMEM)
    return pl.pallas_call(
        blend_kernel,
        out_shape=jax.ShapeDtypeStruct((co.shape[0], side, side), f32),
        in_specs=[pl.BlockSpec(memory_space=pltpu.SMEM)] + [vm] * 5,
        out_specs=vm,
        compiler_params=pltpu.CompilerParams(vmem_limit_bytes=8 << 20),
        name="blend",
    )(odd, co, *strips)


def swap(value, axis, bit):
    count = lax.axis_size(axis)
    return lax.ppermute(value, axis, [(i, i ^ bit) for i in range(count)])


def between(value, axis):
    count = lax.axis_size(axis)
    pairs = [(i, i + 1) for i in range(1, count - 1, 2)]
    return lax.ppermute(value, axis, pairs + [(j, i) for i, j in pairs])


def hop_two(value):
    count = lax.axis_size("sky")
    pairs = [(i, i + 2) for i in range(0, count - 2, 2)] + [(i, i - 2) for i in range(3, count, 2)]
    return lax.ppermute(value, "sky", pairs)


def local(features, target, images, layer_mask, pair_list, ridge_weight):
    npix, feat = features.shape[2:]
    layers = images.shape[2]
    nout = target.shape[2]
    side = int(round(nout**0.5))
    shapes = (npix, layers, nout, side, feat)
    sky_at, batch_at = lax.axis_index("sky"), lax.axis_index("batch")
    own = pack(features, images, layer_mask)
    n0 = swap(own, "sky", 1)
    a2 = swap(own, "batch", 2)
    a1 = swap(own, "batch", 1)
    t2 = halve(target)
    chosen = pair_list.reshape(-1)
    odd = sky_at % 2
    tiles = jnp.asarray(TILE, jnp.int32)
    column = jnp.where(tiles == 0, 1, jnp.where((tiles == 1) == (odd == 0), 2, 0))
    names = 3 * (jnp.asarray(FLIP, jnp.int32) ^ batch_at) + column
    match = (names[:, None] == chosen[None, :]).astype(jnp.int32)
    hit = jnp.sum(match, axis=1)
    order = jnp.arange(names.shape[0])
    count = jnp.sum(jnp.where(order[None, :] < order[:, None], hit[None, :], 0), axis=1)
    rank = jnp.where(hit > 0, count, -1).astype(jnp.int32)
    pos = jnp.sum(match * count[:, None], axis=0).astype(jnp.int32)
    parity = jnp.stack([odd, batch_at % 2]).astype(jnp.int32)

    masks = jnp.asarray(fade_masks(nout, side))
    common = (rank, ridge_weight, parity, masks)
    d0 = hop_two(n0)
    n2 = swap(n0, "batch", 2)
    a3 = swap(a2, "batch", 1)
    n1 = swap(n0, "batch", 1)
    arrs = [own, a1, a2, n0, a3, n1]
    fa_h, fa_l, p, w, ia = phase(0, *common, arrs, t2, [], None, [], shapes)
    n2, d0, fa_h = lax.optimization_barrier((n2, d0, fa_h))
    d2 = swap(d0, "batch", 2)
    n3 = swap(n2, "batch", 1)
    d1 = swap(d0, "batch", 1)
    arrs += [n2, d0, n3]
    fb_h, fb_l, p, w, ib = phase(1, *common, arrs, t2, [(fa_h, fa_l)], (p, w), [], shapes)
    d2, fb_h = lax.optimization_barrier((d2, fb_h))
    d3 = swap(d2, "batch", 1)
    arrs += [d1, d2, d3]
    olds = [(fa_h, fa_l), (fb_h, fb_l)]
    z, v, co, near, far, pair, mid = phase(
        2, *common, arrs, t2, olds, (p, w), [ia, ib], shapes
    )
    near = swap(near, "sky", 1)
    far = between(far, "sky")
    pair = swap(pair, "batch", 1)
    mid = between(mid, "batch")
    transfer = close(pos, w, v, z)
    image = blend(parity, co, (near, far, pair, mid), side)
    return (transfer.reshape(1, 1, -1, nout), image)


def solution(mesh):
    in_specs = (
        P("batch", "sky", None, None),
        P("batch", "sky", None, None),
        P("batch", "sky", None, None),
        P("batch", "sky", None),
        P("batch", "sky", None),
        P("batch", "sky"),
    )
    out_specs = (P("batch", "sky", None, None), P(None, "batch", "sky"))
    return jax.shard_map(local, mesh=mesh, in_specs=in_specs, out_specs=out_specs, check_vma=False)
```

```python
import functools

import jax
import jax.numpy as jnp
import numpy as np
from jax import lax
from jax.experimental import pallas as pl
from jax.experimental.pallas import tpu as pltpu
from jax.sharding import PartitionSpec as P

f32 = jnp.float32
bf16 = jnp.bfloat16
LANE = 128
SUB = 8
FADE = 4
PHASES = (3, 3, 3)
ARRIVED = (6, 10, 12)
FLIP = (0, 1, 2, 0, 3, 1, 2, 0, 3, 1, 2, 3)
TILE = (0, 0, 0, 1, 0, 1, 1, 2, 1, 2, 2, 2)


def split2(x):
    hi = x.astype(bf16)
    lo = (x - hi.astype(f32)).astype(bf16)
    return hi, lo


def dot(a, b, tb=False):
    dims = (((1,), (1 if tb else 0,)), ((), ()))
    return lax.dot_general(a, b, dims, preferred_element_type=f32)


def dot3(a, b, tb=False):
    return dot(a[0], b[0], tb) + (dot(a[0], b[1], tb) + dot(a[1], b[0], tb))


def panel_sweep(rows, q, sub, lane):
    base = q * SUB
    p = rows[q]
    wide = lambda x: jnp.broadcast_to(x, (SUB, LANE))
    cols = [jnp.where(lane >= 0, wide(p[:, base + k : base + k + 1]), 0.0) for k in range(SUB)]
    inside = (lane >= base) & (lane < base + SUB)
    w = jnp.where(inside, jnp.where(lane - base == sub, 1.0, 0.0).astype(f32), p)
    for k in range(0, SUB, 2):
        first, second = sub == k, sub == k + 1
        both = first | second
        a, d = wide(cols[k][k : k + 1]), wide(cols[k][k + 1 : k + 2])
        b, c = wide(cols[k + 1][k : k + 1]), wide(cols[k + 1][k + 1 : k + 2])
        r = 1.0 / (a * c - b * d)
        h1 = jnp.where(first, -1.0, jnp.where(second, 0.0, cols[k]))
        h2 = jnp.where(second, -1.0, jnp.where(first, 0.0, cols[k + 1]))

        def step(x):
            r1, r2 = wide(x[k : k + 1]), wide(x[k + 1 : k + 2])
            t = h1 * (c * r1 - b * r2) + h2 * (a * r2 - d * r1)
            return jnp.where(both, 0.0, x) - t * r

        for m in range(k + 2, SUB):
            cols[m] = step(cols[m])
        w = step(w)
    wk = [wide(w[k : k + 1]) for k in range(SUB)]
    count = len(rows)
    res = [None] * count
    for step_at in range(count):
        g = (q + 1 + step_at) % count
        if g == q:
            res[g] = w
            continue
        x = rows[g]
        terms = [wide(x[:, base + k : base + k + 1]) * wk[k] for k in range(SUB)]
        while len(terms) > 1:
            terms = [terms[i] + terms[i + 1] for i in range(0, len(terms), 2)]
        res[g] = jnp.where(inside, 0.0, x) - terms[0]
    return res


def pack_kernel(mask_ref, feat_in, img_in, out_ref, img_ref, sems):
    npix, feat = feat_in.shape[2:]
    layers = img_ref.shape[0]
    blocks = feat // LANE
    first = pltpu.make_async_copy(img_in.at[0, 0], img_ref, sems.at[blocks])
    first.start()
    loads = [
        pltpu.make_async_copy(
            feat_in.at[0, 0, :, pl.ds(c * LANE, LANE)],
            out_ref.at[pl.ds(c * npix, npix)],
            sems.at[c],
        )
        for c in range(blocks)
    ]
    for cp in loads:
        cp.start()
    row = lax.broadcasted_iota(jnp.int32, (layers, npix), 0)
    keep = jnp.zeros((layers, npix), f32)
    for i in range(layers):
        keep = jnp.where(row == i, mask_ref[0, 0, i].astype(f32), keep)
    tail = blocks * npix
    out_ref[tail : tail + layers, :] = jnp.zeros((layers, LANE), f32)
    first.wait()
    out_ref[tail : tail + layers, 0:npix] = img_ref[...] * keep
    for cp in loads:
        cp.wait()


def pack(features, images, layer_mask):
    npix, feat = features.shape[2:]
    layers = images.shape[2]
    vm = pl.BlockSpec(memory_space=pltpu.VMEM)
    hb = pl.BlockSpec(memory_space=pltpu.HBM)
    outside = lambda x: pltpu.with_memory_space_constraint(x, pltpu.HBM)
    return pl.pallas_call(
        pack_kernel,
        out_shape=jax.ShapeDtypeStruct((feat // LANE * npix + layers, LANE), f32),
        in_specs=[pl.BlockSpec(memory_space=pltpu.SMEM), hb, hb],
        out_specs=vm,
        scratch_shapes=[
            pltpu.VMEM((layers, npix), f32),
            pltpu.SemaphoreType.DMA((feat // LANE + 1,)),
        ],
        compiler_params=pltpu.CompilerParams(vmem_limit_bytes=8 << 20),
        name="pack",
    )(outside(layer_mask), outside(features), outside(images))


def halve_kernel(t_ref, hi_ref, lo_ref):
    hi, lo = split2(t_ref[0, 0])
    hi_ref[...] = hi
    lo_ref[...] = lo


def halve(target):
    nout, feat = target.shape[2:]
    vm = pl.BlockSpec(memory_space=pltpu.VMEM)
    shape = jax.ShapeDtypeStruct((nout, feat), bf16)
    return pl.pallas_call(
        halve_kernel,
        out_shape=(shape, shape),
        in_specs=[vm],
        out_specs=(vm, vm),
        compiler_params=pltpu.CompilerParams(vmem_limit_bytes=16 << 20),
        name="halve",
    )(target)


def stack_left(x):
    hi, lo = split2(x)
    return jnp.concatenate([hi, hi, lo], axis=1)


def stack_right(x):
    hi, lo = split2(x)
    return jnp.concatenate([hi, lo, hi], axis=0)


def chunks(width, step=256):
    return [slice(at, min(at + step, width)) for at in range(0, width, step)]


def phase_kernel(*refs, done, narr, last, npix, layers, nout, side):
    refs = list(refs)
    take = lambda count: [refs.pop(0) for _ in range(count)]
    rank_ref, ridge_ref, odd_ref = take(3)
    if last:
        (mask_ref,) = take(1)
    arrs = dict(zip(range(sum(done), narr), take(narr - sum(done))))
    th, tl = take(2)
    old = [tuple(take(2)) for _ in done]
    old_p, old_w = take(2) if done else (None, None)
    e = sum(done)
    old_img = take(len(done)) if last else []
    if last:
        r_ref, v_ref, co_ref, near_ref, far_ref, pair_ref, mid_ref = take(7)
        fh_ref, fl_ref, s_ref, d_ref, img_ref = take(5)
    else:
        fh_ref, fl_ref, p_ref, w_ref, img_ref = take(5)
        s_ref, d_ref, r_ref = take(3)
        if done:
            (v_ref,) = take(1)
    n = fh_ref.shape[0]
    l = n // npix
    before = e * npix
    feat_blocks = fh_ref.shape[1] // LANE
    body = feat_blocks * npix

    for t in arrs:
        r = rank_ref[t]

        @pl.when((r >= e) & (r < e + l))
        def _():
            to = pl.ds(pl.multiple_of((r - e) * npix, 2 * SUB), npix)
            for c in range(feat_blocks):
                hi, lo = split2(arrs[t][c * npix : (c + 1) * npix, :])
                fh_ref[to, c * LANE : (c + 1) * LANE] = hi
                fl_ref[to, c * LANE : (c + 1) * LANE] = lo
            img_ref[r - e] = arrs[t][body : body + layers, :]


    mine_h, mine_l = fh_ref[...], fl_ref[...]
    ridge = ridge_ref[0, 0]
    sub = lax.broadcasted_iota(jnp.int32, (SUB, LANE), 0)
    lane = lax.broadcasted_iota(jnp.int32, (SUB, LANE), 1)
    pieces = []
    for xh, xl in old + [(fh_ref, fl_ref)]:
        xh, xl = xh[...], xl[...]
        both = dot(jnp.concatenate([xh, xl], axis=0), mine_h, True)
        pieces.append(both[: xh.shape[0]] + (both[xh.shape[0] :] + dot(xh, mine_l, True)))
    system = pieces[-1]
    cross = []
    if done:
        tops = [sum(done[:i]) * npix for i in range(len(done) + 1)]
        gel = jnp.concatenate(pieces[:-1], axis=0)
        v = dot3(split2(old_p[...]), split2(gel))
        v_ref[...] = v
        for i in range(len(done)):
            rows = slice(tops[i], tops[i + 1])
            cross.append((rows, split2(gel[rows].T)))
        for rows, g in cross:
            system = system - dot3(g, split2(v[rows]))
    d_ref[:, 0:npix] = system[0:npix, 0:npix]
    for c in range(l):
        s_ref[c, :, 0:npix] = system[:, c * npix : (c + 1) * npix]

    work = []
    feat = feat_blocks * LANE

    def right_sides(cut, deep, fresh):
        part = dot3(
            (fh_ref[:, deep], fl_ref[:, deep]), (th[cut, deep], tl[cut, deep]), True
        )
        r_ref[:, cut] = part if fresh else r_ref[:, cut] + part

    def cross_right(cut, rows, g):
        r_ref[:, cut] = r_ref[:, cut] - dot3(g, split2(old_w[rows, cut]))

    for cut in chunks(nout):
        for deep in chunks(feat, feat):
            work.append(functools.partial(right_sides, cut, deep, deep.start == 0))
        for rows, g in cross:
            work.append(functools.partial(cross_right, cut, rows, g))

    picture = {}
    if last:
        faces = [ref[i][:, 0:npix] for ref, count in zip(old_img, done) for i in range(count)]
        faces += [img_ref[i][:, 0:npix] for i in range(l)]

        def base(cut):
            total = None
            for i in range(e):
                part = dot(
                    stack_left(faces[i]), stack_right(old_w[i * npix : (i + 1) * npix, cut])
                )
                total = part if total is None else total + part
            picture[cut.start] = total

        def effective():
            ours = jnp.concatenate(faces[e:], axis=1)
            for i in range(e):
                ours = ours - dot(
                    stack_left(faces[i]), stack_right(v_ref[i * npix : (i + 1) * npix, :])
                )
            picture["rest"] = split2(ours)

        later = [functools.partial(base, cut) for cut in chunks(nout)] + [effective]
    else:
        later = []

    def update(c, coef, d, j):
        rows = slice(j * npix, (j + 1) * npix)
        w = dot(d, stack_right(s_ref[c, rows, 0:npix]))
        s_ref[c, :, 0:npix] = s_ref[c, :, 0:npix] - dot(coef, stack_right(w))
        s_ref[c, rows, 0:npix] = w

    def update_right(coef, d, j, cut):
        rows = slice(j * npix, (j + 1) * npix)
        w = dot(d, stack_right(r_ref[rows, cut]))
        r_ref[:, cut] = r_ref[:, cut] - dot(coef, stack_right(w))
        r_ref[rows, cut] = w

    def update_own(coef, full, j):
        rows = slice(j * npix, (j + 1) * npix)
        s_ref[j, :, 0:npix] = -dot(coef, stack_right(full))
        s_ref[j, rows, 0:npix] = full

    for j in range(l):
        cut = slice(j * npix, (j + 1) * npix)
        after = slice((j + 1) * npix, (j + 2) * npix)
        rows = []
        for g in range(npix // SUB):
            at_row = slice(g * SUB, (g + 1) * SUB)
            rows.append(d_ref[at_row, :] + jnp.where(lane == sub + g * SUB, ridge, 0.0))
        count = len(rows)
        for q in range(count):
            rows = panel_sweep(rows, q, sub, lane)
            for _ in range(-(-len(work) // (count - q))):
                work.pop(0)()
        while work:
            work.pop(0)()
        full = jnp.concatenate(rows, axis=0)[:, :npix]
        if j + 1 < l:
            w = dot3(split2(full), split2(s_ref[j + 1, cut, 0:npix]))
            step = dot3(split2(s_ref[j, after, 0:npix]), split2(w))
            d_ref[:, 0:npix] = s_ref[j + 1, after, 0:npix] - step
        d = stack_left(full)
        coef = stack_left(s_ref[j, :, 0:npix])
        for c in list(range(j + 1, l)) + list(range(j)):
            if c > j or not last:
                work.append(functools.partial(update, c, coef, d, j))
        for part in chunks(nout):
            work.append(functools.partial(update_right, coef, d, j, part))
        if not last:
            work.append(functools.partial(update_own, coef, full, j))
        work += later
        later = []
    while work:
        work.pop(0)()
    z = r_ref[...]
    z2 = split2(z)
    if last:
        base_total = jnp.concatenate([picture[cut.start] for cut in chunks(nout)], axis=1)
        total = base_total + dot3(picture["rest"], z2)
        send(total, co_ref, near_ref, far_ref, pair_ref, mid_ref, mask_ref, odd_ref, side)
        return
    q_flat = jnp.concatenate([s_ref[c, :, 0:npix] for c in range(l)], axis=1)
    w_ref[before : before + n, :] = z
    if done:
        v2 = split2(v_ref[...])
        w_ref[0:before, :] = old_w[...] - dot3(v2, z2)
        q2 = split2(q_flat)
        vq = dot3(v2, q2)
        second = dot3(q2, v2, True)
        first = old_p[...] + dot3(split2(vq), v2, True)
        p_ref[0:before, :] = jnp.concatenate([first, -vq], axis=1)
        p_ref[before : before + n, :] = jnp.concatenate([-second, q_flat], axis=1)
    else:
        p_ref[...] = q_flat


def send(total, co_ref, near_ref, far_ref, pair_ref, mid_ref, mask_ref, odd_ref, side):
    layers, nout = total.shape
    rest = side - FADE
    span = FADE * side
    co_ref[...] = total
    none = jnp.zeros((layers, rest), f32)
    to_west = jnp.concatenate([none, total[:, : nout - rest]], axis=1) * mask_ref[0:1, :]
    to_east = jnp.concatenate([total[:, rest:], none], axis=1) * mask_ref[1:2, :]
    to_north = total[:, 0:span] * mask_ref[2:3, 0:span]
    to_south = total[:, nout - span :] * mask_ref[3:4, 0:span]
    sky_odd, batch_odd = odd_ref[0] == 1, odd_ref[1] == 1
    near_ref[...] = jnp.where(sky_odd, to_west, to_east)
    far_ref[...] = jnp.where(sky_odd, to_east, to_west)
    pair_ref[...] = jnp.where(batch_odd, to_north, to_south)
    mid_ref[...] = jnp.where(batch_odd, to_south, to_north)


def fade_masks(nout, side):
    ramp = (np.arange(FADE, dtype=np.float32) + np.float32(1.0)) / np.float32(FADE + 1.0)
    column = np.arange(nout) % side
    rest = side - FADE
    masks = np.zeros((4, nout), np.float32)
    masks[0] = np.where(column >= rest, ramp[np.maximum(column - rest, 0)], 0.0)
    masks[1] = np.where(column < FADE, ramp[::-1][np.minimum(column, FADE - 1)], 0.0)
    masks[2, : FADE * side] = np.repeat(ramp, side)
    masks[3, : FADE * side] = np.repeat(ramp[::-1], side)
    return masks


def phase(number, rank, ridge, odd, masks, arrs, t2, old, state, faces, shapes):
    npix, layers, nout, side, feat = shapes
    done = PHASES[:number]
    l = PHASES[number]
    last = number == len(PHASES) - 1
    e = sum(done)
    n, size = l * npix, (e + l) * npix
    vm = pl.BlockSpec(memory_space=pltpu.VMEM)
    sm = pl.BlockSpec(memory_space=pltpu.SMEM)
    args = [rank, ridge, odd]
    specs = [sm, sm, sm]
    if last:
        args += [masks]
    args += list(arrs[e:]) + list(t2)
    for pair in old:
        args += list(pair)
    if done:
        args += list(state)
    if last:
        args += list(faces)
    specs += [vm] * (len(args) - len(specs))
    real = lambda *shape: jax.ShapeDtypeStruct(shape, f32)
    half = jax.ShapeDtypeStruct((n, feat), bf16)
    if last:
        outs = (
            real(n, nout),
            real(e * npix, n),
            real(layers, nout),
            real(layers, nout),
            real(layers, nout),
            real(layers, FADE * side),
            real(layers, FADE * side),
        )
        scratch = [pltpu.VMEM((n, feat), bf16)] * 2
    else:
        outs = (half, half, real(size, size), real(size, nout), real(l, layers, LANE))
        scratch = []
    scratch += [pltpu.VMEM((l, n, LANE), f32), pltpu.VMEM((npix, LANE), f32)]
    if last:
        scratch += [pltpu.VMEM((l, layers, LANE), f32)]
    else:
        scratch += [pltpu.VMEM((n, nout), f32)]
        if done:
            scratch += [pltpu.VMEM((e * npix, n), f32)]
    out_specs = tuple(vm for _ in outs)
    return pl.pallas_call(
        functools.partial(
            phase_kernel,
            done=done,
            narr=len(arrs),
            last=last,
            npix=npix,
            layers=layers,
            nout=nout,
            side=side,
        ),
        out_shape=outs,
        in_specs=specs,
        out_specs=out_specs,
        scratch_shapes=scratch,
        compiler_params=pltpu.CompilerParams(vmem_limit_bytes=16 << 20),
        cost_estimate=pl.CostEstimate(
            flops=2_000_000_000 * l, transcendentals=0, bytes_accessed=4_000_000
        ),
        name="phase%d" % number,
    )(*args)


def close_kernel(pos_ref, w_ref, v_ref, z_ref, out_ref):
    before = w_ref.shape[0]
    n = z_ref.shape[0]
    count = pos_ref.shape[0]
    npix = (before + n) // count
    z = z_ref[...]
    front = w_ref[...] - dot3(split2(v_ref[...]), split2(z))
    for r in range(count):
        to = sum(jnp.where(pos_ref[k] == r, k, 0) for k in range(count))
        top = r * npix
        block = front[top : top + npix] if top < before else z[top - before : top - before + npix]
        out_ref[pl.ds(pl.multiple_of(to * npix, SUB), npix), :] = block


def close(pos, w, v, z):
    before, nout = w.shape
    n = z.shape[0]
    vm = pl.BlockSpec(memory_space=pltpu.VMEM)
    return pl.pallas_call(
        close_kernel,
        out_shape=jax.ShapeDtypeStruct((before + n, nout), f32),
        in_specs=[pl.BlockSpec(memory_space=pltpu.SMEM), vm, vm, vm],
        out_specs=vm,
        compiler_params=pltpu.CompilerParams(vmem_limit_bytes=20 << 20),
        cost_estimate=pl.CostEstimate(
            flops=500_000_000, transcendentals=0, bytes_accessed=6_000_000
        ),
        name="close",
    )(pos, w, v, z)


def blend_kernel(odd_ref, co_ref, near_ref, far_ref, pair_ref, mid_ref, out_ref):
    layers, side, _ = out_ref.shape
    nout = co_ref.shape[1]
    span = FADE * side
    batch_odd = odd_ref[1] == 1
    pair, mid = pair_ref[...], mid_ref[...]
    south = jnp.where(batch_odd, mid, pair)
    north = jnp.where(batch_odd, pair, mid)
    none = jnp.zeros((layers, nout - 2 * span), f32)
    total = co_ref[...] + near_ref[...] + far_ref[...] + jnp.concatenate([north, none, south], axis=1)
    for r in range(side):
        out_ref[:, r, :] = total[:, r * side : (r + 1) * side]


def blend(odd, co, strips, side):
    vm = pl.BlockSpec(memory_space=pltpu.VMEM)
    return pl.pallas_call(
        blend_kernel,
        out_shape=jax.ShapeDtypeStruct((co.shape[0], side, side), f32),
        in_specs=[pl.BlockSpec(memory_space=pltpu.SMEM)] + [vm] * 5,
        out_specs=vm,
        compiler_params=pltpu.CompilerParams(vmem_limit_bytes=8 << 20),
        name="blend",
    )(odd, co, *strips)


def swap(value, axis, bit):
    count = lax.axis_size(axis)
    return lax.ppermute(value, axis, [(i, i ^ bit) for i in range(count)])


def between(value, axis):
    count = lax.axis_size(axis)
    pairs = [(i, i + 1) for i in range(1, count - 1, 2)]
    return lax.ppermute(value, axis, pairs + [(j, i) for i, j in pairs])


def hop_two(value):
    count = lax.axis_size("sky")
    pairs = [(i, i + 2) for i in range(0, count - 2, 2)] + [(i, i - 2) for i in range(3, count, 2)]
    return lax.ppermute(value, "sky", pairs)


def local(features, target, images, layer_mask, pair_list, ridge_weight):
    npix, feat = features.shape[2:]
    layers = images.shape[2]
    nout = target.shape[2]
    side = int(round(nout**0.5))
    shapes = (npix, layers, nout, side, feat)
    sky_at, batch_at = lax.axis_index("sky"), lax.axis_index("batch")
    own = pack(features, images, layer_mask)
    n0 = swap(own, "sky", 1)
    a2 = swap(own, "batch", 2)
    a1 = swap(own, "batch", 1)
    t2 = halve(target)
    chosen = pair_list.reshape(-1)
    odd = sky_at % 2
    tiles = jnp.asarray(TILE, jnp.int32)
    column = jnp.where(tiles == 0, 1, jnp.where((tiles == 1) == (odd == 0), 2, 0))
    names = 3 * (jnp.asarray(FLIP, jnp.int32) ^ batch_at) + column
    match = (names[:, None] == chosen[None, :]).astype(jnp.int32)
    hit = jnp.sum(match, axis=1)
    order = jnp.arange(names.shape[0])
    count = jnp.sum(jnp.where(order[None, :] < order[:, None], hit[None, :], 0), axis=1)
    rank = jnp.where(hit > 0, count, -1).astype(jnp.int32)
    pos = jnp.sum(match * count[:, None], axis=0).astype(jnp.int32)
    parity = jnp.stack([odd, batch_at % 2]).astype(jnp.int32)

    masks = jnp.asarray(fade_masks(nout, side))
    common = (rank, ridge_weight, parity, masks)
    d0 = hop_two(n0)
    n2 = swap(n0, "batch", 2)
    a3 = swap(a2, "batch", 1)
    n1 = swap(n0, "batch", 1)
    arrs = [own, a1, a2, n0, a3, n1]
    fa_h, fa_l, p, w, ia = phase(0, *common, arrs, t2, [], None, [], shapes)
    n2, d0, fa_h = lax.optimization_barrier((n2, d0, fa_h))
    d2 = swap(d0, "batch", 2)
    n3 = swap(n2, "batch", 1)
    d1 = swap(d0, "batch", 1)
    arrs += [n2, d0, n3]
    fb_h, fb_l, p, w, ib = phase(1, *common, arrs, t2, [(fa_h, fa_l)], (p, w), [], shapes)
    d2, fb_h = lax.optimization_barrier((d2, fb_h))
    d3 = swap(d2, "batch", 1)
    arrs += [d1, d2, d3]
    olds = [(fa_h, fa_l), (fb_h, fb_l)]
    z, v, co, near, far, pair, mid = phase(
        2, *common, arrs, t2, olds, (p, w), [ia, ib], shapes
    )
    near = swap(near, "sky", 1)
    far = between(far, "sky")
    pair = swap(pair, "batch", 1)
    mid = between(mid, "batch")
    transfer = close(pos, w, v, z)
    image = blend(parity, co, (near, far, pair, mid), side)
    return (transfer.reshape(1, 1, -1, nout), image)


def solution(mesh):
    in_specs = (
        P("batch", "sky", None, None),
        P("batch", "sky", None, None),
        P("batch", "sky", None, None),
        P("batch", "sky", None),
        P("batch", "sky", None),
        P("batch", "sky"),
    )
    out_specs = (P("batch", "sky", None, None), P(None, "batch", "sky"))
    return jax.shard_map(local, mesh=mesh, in_specs=in_specs, out_specs=out_specs, check_vma=False)
```
